1024 devices in a mesh: section: 128 (over z, y_hi, core), dp: 8 (over y_lo, x).
Axes of the slice: x: 4, y: 4 (y_hi: 2, y_lo: 2; y = y_hi * 2 + y_lo), z: 32, core: 2. Of those that a mesh axis runs over, the one named last changes fastest.
Arguments:
- w_up: bfloat16 [128, 32, 128, 128], P('section'), may hold values from -0.375 to 0.375
- up_index: int32 [128, 32], P('section'), may hold values from 0 to 31
- w_down: bfloat16 [128, 32, 128, 128], P('section'), may hold values from -0.375 to 0.375
- down_index: int32 [128, 32], P('section'), may hold values from 0 to 31
- tick_order: int32 [128, 2], P('section'), may hold values from 0 to 1, each once within a row
- values_in: bfloat16 [128, 64, 4096], P('section', 'dp'), may hold values from -6 to 6
- score_grad_in: bfloat16 [128, 64, 4096], P('section', 'dp'), may hold values from -6 to 6
- tangent_in: bfloat16 [128, 64, 4096], P('section', 'dp'), may hold values from -6 to 6
- state_adjoint_in: bfloat16 [128, 64, 4096], P('section', 'dp'), may hold values from -6 to 6
- saved_back: bfloat16 [128, 2, 64, 4096], P('section', None, 'dp'), may hold values from -6 to 6
- saved_tan: bfloat16 [128, 2, 64, 4096], P('section', None, 'dp'), may hold values from -6 to 6
- saved_second: bfloat16 [128, 2, 64, 4096], P('section', None, 'dp'), may hold values from -6 to 6
- saved_second_tan: bfloat16 [128, 2, 64, 4096], P('section', None, 'dp'), may hold values from -6 to 6
- saved_second_grad: bfloat16 [128, 2, 64, 4096], P('section', None, 'dp'), may hold values from -6 to 6
Outputs:
- values_out: bfloat16 [128, 64, 4096], P('section', 'dp')
- score_grad_out: bfloat16 [128, 64, 4096], P('section', 'dp')
- tangent_out: bfloat16 [128, 64, 4096], P('section', 'dp')
- state_adjoint_out: bfloat16 [128, 64, 4096], P('section', 'dp')
- grad_up: bfloat16 [128, 32, 128, 128], P('section', 'dp')
- grad_down: bfloat16 [128, 32, 128, 128], P('section', 'dp')
The draws below stay inside these ranges and needn't reach their ends.
Inputs may be any that keep to these rules, and one draw needn't show every extreme that they name: up_index[s, j] is the input block that hidden block j of layer s reads. down_index[s, i] is the hidden block that output block i of layer s reads. `tick_order`: each row is a permutation of the 2 slots.
All inputs are finite; a program needn't handle non-finite values.
Results may differ from the reference program's by a relative error of at most 0.023.
Values may be sent and summed in bfloat16 or wider, within the bound.
A program may use at most 32 MiB of HBM per device.

```python
import jax
import jax.numpy as jnp
from jax import lax

D = 4096
BLOCK = 128
TICKS = 2
LAYERS = 128
ROWS = 64
DB = 32
FB = 32
N_DP = 8


def touch_ends(drawn, rng, smallest, top_value):
    spot = [jax.random.randint(jax.random.fold_in(rng, axis), (), 0, length) for axis, length in enumerate(drawn.shape)]
    longest = drawn.shape.index(max(drawn.shape))
    neighbour = spot[:longest] + [(spot[longest] + 1) % drawn.shape[longest]] + spot[longest + 1:]
    return drawn.at[tuple(spot)].set(smallest).at[tuple(neighbour)].set(top_value)


def shard_levels(key, shape, split, least, high):
    gain, own = 1.0, jax.random.fold_in(key, 6)
    for dim, blocks in split:
        heights = jnp.exp(jax.random.uniform(jax.random.fold_in(own, dim), (blocks,), jnp.float32, least / len(split), high / len(split)))
        gain = gain * jnp.repeat(heights, shape[dim] // blocks).reshape([-1 if axis == dim else 1 for axis in range(len(shape))])
    return gain


def gaussian(rng, dims, scale, bound, cuts=(), held_as=jnp.bfloat16):
    array = jax.random.normal(rng, dims, jnp.float32) * scale
    if len(cuts) > 0:
        array = shard_levels(rng, dims, cuts, -0.22, 0.18) * array
    return jnp.clip(array, min=-bound, max=bound).astype(held_as)


def setup_inputs(seed: int = 0) -> dict:
    key_list = jax.random.split(jax.random.key(seed), 15)
    w_up = gaussian(key_list[0], (LAYERS, FB, BLOCK, BLOCK), (2 * BLOCK) ** -0.5, 0.375, ((0, 128),))
    up_index = touch_ends(jax.random.randint(key_list[1], (LAYERS, FB), 0, DB), jax.random.fold_in(key_list[1], 1), 0, DB - 1).astype(jnp.int32)
    w_down = gaussian(key_list[2], (LAYERS, DB, BLOCK, BLOCK), (2 * BLOCK) ** -0.5, 0.375, ((0, 128),))
    down_index = touch_ends(jax.random.randint(key_list[3], (LAYERS, DB), 0, FB), jax.random.fold_in(key_list[3], 1), 0, FB - 1).astype(jnp.int32)
    tick_order = jax.vmap(lambda own: jax.random.permutation(own, TICKS))(jax.random.split(key_list[4], LAYERS)).reshape((LAYERS, TICKS)).astype(jnp.int32)
    values_in = gaussian(key_list[5], (LAYERS, ROWS, D), 1.0, 6.0, ((0, 128), (1, 8)))
    score_grad_in = gaussian(key_list[6], (LAYERS, ROWS, D), 1.0, 6.0, ((0, 128), (1, 8)))
    tangent_in = gaussian(key_list[7], (LAYERS, ROWS, D), 1.0, 6.0, ((0, 128), (1, 8)))
    state_adjoint_in = gaussian(key_list[8], (LAYERS, ROWS, D), 1.0, 6.0, ((0, 128), (1, 8)))
    saved_back = gaussian(key_list[9], (LAYERS, TICKS, ROWS, D), 1.0, 6.0, ((0, 128), (2, 8)))
    saved_tan = gaussian(key_list[10], (LAYERS, TICKS, ROWS, D), 1.0, 6.0, ((0, 128), (2, 8)))
    saved_second = gaussian(key_list[11], (LAYERS, TICKS, ROWS, D), 1.0, 6.0, ((0, 128), (2, 8)))
    saved_second_tan = gaussian(key_list[12], (LAYERS, TICKS, ROWS, D), 1.0, 6.0, ((0, 128), (2, 8)))
    saved_second_grad = gaussian(key_list[13], (LAYERS, TICKS, ROWS, D), 1.0, 6.0, ((0, 128), (2, 8)))
    return dict(w_up=w_up, up_index=up_index, w_down=w_down, down_index=down_index, tick_order=tick_order, values_in=values_in, score_grad_in=score_grad_in, tangent_in=tangent_in, state_adjoint_in=state_adjoint_in, saved_back=saved_back, saved_tan=saved_tan, saved_second=saved_second, saved_second_tan=saved_second_tan, saved_second_grad=saved_second_grad)


def silu_parts(inputs):
    logistic = jax.nn.sigmoid(inputs)
    slopes = logistic * (1.0 + inputs * (1.0 - logistic))
    curves = logistic * (1.0 - logistic) * (2.0 + inputs * (1.0 - 2.0 * logistic))
    return (inputs * logistic, slopes, curves)

def block_map(matrix, weight, block_table):
    block_width = weight.shape[-1]
    row_count = matrix.shape[0]
    pieces = matrix.astype(jnp.float32).reshape(row_count, -1, block_width)
    picked = jnp.take(pieces, block_table, axis=1)
    result = jnp.einsum('rnk,nkj->rnj', picked, weight.astype(jnp.float32), precision=lax.Precision.HIGHEST)
    return result.reshape(row_count, -1)

def block_map_back(matrix, weight, block_table, block_count):
    block_width = weight.shape[-1]
    row_count = matrix.shape[0]
    pieces = matrix.astype(jnp.float32).reshape(row_count, -1, block_width)
    partial_value = jnp.einsum('rnj,nkj->rnk', pieces, weight.astype(jnp.float32), precision=lax.Precision.HIGHEST)
    placing = (block_table[:, None] == jnp.arange(block_count, dtype=jnp.int32)[None, :]).astype(jnp.float32)
    result = jnp.einsum('rnk,nc->rck', partial_value, placing, precision=lax.Precision.HIGHEST)
    return result.reshape(row_count, -1)

def layer_tick(params, streams, saved):
    up_weight, up_table, down_weight, down_table = params
    values, score_grad, tangent, adjoint = streams
    back_input, tangent_input, second_input, second_tangent, second_grad = saved
    hidden_blocks = up_weight.shape[0]
    model_blocks = down_weight.shape[0]
    hidden_values = silu_parts(block_map(values, up_weight, up_table))[0].astype(jnp.bfloat16)
    new_values = (values.astype(jnp.float32) + block_map(hidden_values, down_weight, down_table)).astype(jnp.bfloat16)
    active_back, slope_back, unused_curve = silu_parts(block_map(back_input, up_weight, up_table))
    hidden_back = active_back.astype(jnp.bfloat16)
    gate_back = (slope_back * block_map_back(score_grad, down_weight, down_table, hidden_blocks)).astype(jnp.bfloat16)
    new_score_grad = (score_grad.astype(jnp.float32) + block_map_back(gate_back, up_weight, up_table, model_blocks)).astype(jnp.bfloat16)
    tangent_slope = silu_parts(block_map(tangent_input, up_weight, up_table))[1]
    tangent_hidden = (tangent_slope * block_map(tangent, up_weight, up_table)).astype(jnp.bfloat16)
    new_tangent = (tangent.astype(jnp.float32) + block_map(tangent_hidden, down_weight, down_table)).astype(jnp.bfloat16)
    active_second, slope_second, curve_second = silu_parts(block_map(second_input, up_weight, up_table))
    raised_second_tangent = block_map(second_tangent, up_weight, up_table)
    pulled_second = block_map_back(second_grad, down_weight, down_table, hidden_blocks)
    pulled_adjoint = block_map_back(adjoint, down_weight, down_table, hidden_blocks)
    second_push = (slope_second * pulled_adjoint + curve_second * pulled_second * raised_second_tangent).astype(jnp.bfloat16)
    new_adjoint = (adjoint.astype(jnp.float32) + block_map_back(second_push, up_weight, up_table, model_blocks)).astype(jnp.bfloat16)
    hidden_second = active_second.astype(jnp.bfloat16)
    tangent_second = (slope_second * raised_second_tangent).astype(jnp.bfloat16)
    gated_second = (slope_second * pulled_second).astype(jnp.bfloat16)
    up_pairs = ((back_input, gate_back), (second_input, second_push), (second_tangent, gated_second))
    down_pairs = ((hidden_back, score_grad), (hidden_second, adjoint), (tangent_second, second_grad))
    return ((new_values, new_score_grad, new_tangent, new_adjoint), up_pairs, down_pairs)

def pair_grad(inputs, cotangents, block_table, groups):
    row_count = inputs.shape[0]
    pieces = inputs.astype(jnp.float32).reshape(groups, row_count // groups, -1, BLOCK)
    picked = jnp.take(pieces, block_table, axis=2)
    cot_pieces = cotangents.astype(jnp.float32).reshape(groups, row_count // groups, -1, BLOCK)
    return jnp.einsum('grnk,grnj->gnkj', picked, cot_pieces, precision=lax.Precision.HIGHEST)

def reference(w_up, up_index, w_down, down_index, tick_order, values_in, score_grad_in, tangent_in, state_adjoint_in, saved_back, saved_tan, saved_second, saved_second_tan, saved_second_grad):

    def gather_inputs(layer_index, tick_number, streams):
        slot_index = tick_order[layer_index, tick_number]
        params = (w_up[layer_index], up_index[layer_index], w_down[layer_index], down_index[layer_index])
        local = (streams[0][layer_index], streams[1][layer_index], streams[2][layer_index], streams[3][layer_index])
        saved = (saved_back[layer_index, slot_index], saved_tan[layer_index, slot_index], saved_second[layer_index, slot_index], saved_second_tan[layer_index, slot_index], saved_second_grad[layer_index, slot_index])
        return (params, local, saved)
    streams = (values_in, score_grad_in, tangent_in, state_adjoint_in)
    history = []
    for tick_number in range(TICKS):
        history.append(streams)

        def advance(layer_index):
            params, local, saved = gather_inputs(layer_index, tick_number, streams)
            return layer_tick(params, local, saved)[0]
        moved = lax.map(advance, jnp.arange(LAYERS, dtype=jnp.int32))
        streams = (jnp.roll(moved[0], 1, 0), jnp.roll(moved[1], -1, 0), jnp.roll(moved[2], 1, 0), jnp.roll(moved[3], -1, 0))

    def layer_grads(layer_index):
        up_total = jnp.zeros((N_DP, FB, BLOCK, BLOCK), jnp.float32)
        down_total = jnp.zeros((N_DP, DB, BLOCK, BLOCK), jnp.float32)
        for tick_number in range(TICKS):
            params, local, saved = gather_inputs(layer_index, tick_number, history[tick_number])
            unused_streams, up_pairs, down_pairs = layer_tick(params, local, saved)
            for entry in up_pairs:
                up_total = up_total + pair_grad(entry[0], entry[1], up_index[layer_index], N_DP)
            for entry in down_pairs:
                down_total = down_total + pair_grad(entry[0], entry[1], down_index[layer_index], N_DP)
        up_share = lax.optimization_barrier((up_total * (1.0 / ROWS)).astype(jnp.bfloat16))
        down_share = lax.optimization_barrier((down_total * (1.0 / ROWS)).astype(jnp.bfloat16))
        up_sum = lax.optimization_barrier(jnp.sum(up_share.astype(jnp.float32), 0)).astype(jnp.bfloat16)
        down_sum = lax.optimization_barrier(jnp.sum(down_share.astype(jnp.float32), 0)).astype(jnp.bfloat16)
        return (up_sum, down_sum)
    grad_up, grad_down = lax.map(layer_grads, jnp.arange(LAYERS, dtype=jnp.int32))
    return (streams[0], streams[1], streams[2], streams[3], grad_up, grad_down)
```

```python
import functools

import jax
import jax.numpy as jnp
from jax import lax
from jax.experimental import pallas as pl
from jax.experimental.pallas import tpu as pltpu
from jax.sharding import PartitionSpec as P

BLOCK = 128
UNROLL = 8
MESH = pl.DeviceIdType.MESH
F32 = jnp.float32
BF16 = jnp.bfloat16


def logistic(z):
    return 0.5 * jnp.tanh(0.5 * z) + 0.5


def silu_of(z, sig):
    return z * sig


def slope_of(z, sig):
    return sig * (1.0 + z * (1.0 - sig))


def curve_of(z, sig):
    return sig * (1.0 - sig) * (2.0 + z * (1.0 - 2.0 * sig))


def cols(i, width=BLOCK):
    return pl.ds(pl.multiple_of(i * width, width), width)


def each_block(count, body):
    def step(t, carry):
        for u in range(UNROLL):
            body(t * UNROLL + u)
        return carry

    lax.fori_loop(0, count // UNROLL, step, 0)


def dot(a, b):
    return jnp.dot(a, b, preferred_element_type=F32)


def dot_t(a, b):
    return lax.dot_general(a, b, (((1,), (1,)), ((), ())), preferred_element_type=F32)


def tick_kernel(
    n_section, n_dp, blocks, scale,
    up_index, down_index, tick_order, links,
    w_up, w_down, values_in, score_in, tangent_in, adjoint_in,
    saved_back, saved_tan, saved_second, saved_second_tan, saved_second_grad,
    vt_out, ga_out, grads_out,
    wu, wd, raw_x, raw_v, raw_c, x_slots, c_slots, xt, xs, cs,
    v0, v1, g1, v_sent, g_sent, v_last, g_last,
    ys, yy, e0, e1, h0, h1, rx, ry, rc, re,
    chain, chain2, keep,
    in_sem, send_sem, recv_sem, link_send, link_recv,
):
    section = lax.axis_index("section")
    me = lax.axis_index("dp")
    after = lax.rem(section + 1, n_section)
    before = lax.rem(section + n_section - 1, n_section)
    kept = blocks // n_dp

    loads = []

    def load(source, target):
        copy = pltpu.make_async_copy(source, target, in_sem.at[len(loads)])
        copy.start()
        loads.append(copy)

    for slot in range(2):
        for at, saved in enumerate((saved_back, saved_second, saved_second_tan, saved_tan)):
            load(saved.at[0, slot], raw_x.at[slot, pl.ds(8 * at, 8)])
    load(score_in.at[0], raw_c.at[pl.ds(0, 8)])
    load(adjoint_in.at[0], raw_c.at[pl.ds(8, 8)])
    for slot in range(2):
        load(saved_second_grad.at[0, slot], raw_c.at[pl.ds(16 + 8 * slot, 8)])
    early = len(loads)
    load(values_in.at[0], raw_v.at[pl.ds(0, 8)])
    load(tangent_in.at[0], raw_v.at[pl.ds(8, 8)])
    load(w_down.at[0], wd)
    load(w_up.at[0], wu)

    barrier = pltpu.get_barrier_semaphore()
    for p in range(1, n_dp):
        pl.semaphore_signal(barrier, inc=1, device_id={"dp": lax.rem(me + p, n_dp)}, device_id_type=MESH)
    for s in (after, before):
        pl.semaphore_signal(barrier, inc=1, device_id={"section": s}, device_id_type=MESH)

    first = tick_order[0, 0] * blocks
    later = tick_order[0, 1] * blocks

    chain[0] = jnp.zeros(chain.shape[1:], F32)
    chain2[0] = jnp.zeros(chain2.shape[1:], F32)

    for copy in loads[:early]:
        copy.wait()

    def to_blocks(j):
        here = cols(j)
        for slot in range(2):
            x_slots[slot * blocks + j] = raw_x[slot, :, here]
            c_slots[slot * blocks + j] = raw_c[pl.ds(16 + 8 * slot, 8), here]
        cs[j, pl.ds(0, 16)] = raw_c[pl.ds(0, 16), here]

    each_block(blocks, to_blocks)

    def gather_x(j):
        source = up_index[0, j]
        xs[j, pl.ds(0, 24)] = x_slots[first + source, pl.ds(0, 24)]
        xs[j, pl.ds(24, 8)] = x_slots[later + source, pl.ds(16, 8)]
        xs[j, pl.ds(32, 16)] = x_slots[later + source, pl.ds(0, 16)]
        cs[j, pl.ds(16, 8)] = c_slots[first + j]
        cs[j, pl.ds(24, 8)] = c_slots[later + j]

    each_block(blocks, gather_x)
    pl.semaphore_wait(barrier, n_dp + 1)

    sent = []

    def slab(ref, d):
        return ref.at[pl.ds(d * kept, kept)]

    def spread(kind, source, landing):
        for p in range(1, n_dp):
            peer = lax.rem(me + p, n_dp)
            copy = pltpu.make_async_remote_copy(
                src_ref=slab(source, peer),
                dst_ref=landing(me),
                send_sem=send_sem.at[kind, p - 1],
                recv_sem=recv_sem.at[kind, p - 1],
                device_id={"dp": peer},
                device_id_type=MESH,
            )
            copy.start()
            sent.append(copy)

    spread(0, xs, lambda d: rx.at[d])
    spread(1, cs, lambda d: rc.at[d, :, pl.ds(0, 32)])
    rx[me] = xs[pl.ds(me * kept, kept)]
    rc[me, :, pl.ds(0, 32)] = cs[pl.ds(me * kept, kept)]

    for copy in loads[early : early + 2]:
        copy.wait()

    def to_blocks_v(j):
        v0[j] = raw_v[:, cols(j)]

    each_block(blocks, to_blocks_v)

    def gather_v(j):
        source = up_index[0, j]
        xt[j, pl.ds(0, 16)] = v0[source]
        xt[j, pl.ds(16, 8)] = x_slots[first + source, pl.ds(24, 8)]
        xt[j, pl.ds(24, 8)] = x_slots[later + source, pl.ds(24, 8)]

    each_block(blocks, gather_v)
    loads[early + 2].wait()

    def pull(i):
        chain[i + 1] = dot_t(cs[i], wd[i]) + chain[links[0, i]]

    each_block(blocks, pull)
    loads[early + 3].wait()

    def raise_all(j):
        z = dot(jnp.concatenate([xt[j], xs[j]], 0), wu[j])
        zv, zt, tan_f, tan_l = z[0:8], z[8:16], z[16:24], z[24:32]
        back_f, za_f, ta_f = z[32:40], z[40:48], z[48:56]
        ta_l, back_l, za_l = z[56:64], z[64:72], z[72:80]
        pulled = chain[links[2, j]]
        pg, pa, ps_f, ps_l = pulled[0:8], pulled[8:16], pulled[16:24], pulled[24:32]
        sig_f, sig_l = logistic(za_f), logistic(za_l)
        slope_f, slope_l = slope_of(za_f, sig_f), slope_of(za_l, sig_l)
        sig_bf, sig_bl = logistic(back_f), logistic(back_l)
        hidden = silu_of(zv, logistic(zv))
        tangent_hidden = slope_of(tan_f, logistic(tan_f)) * zt
        h0[j] = jnp.concatenate([hidden, tangent_hidden], 0).astype(BF16)
        gate = slope_of(back_f, sig_bf) * pg
        push = slope_f * pa + curve_of(za_f, sig_f) * ps_f * ta_f
        e0[j] = jnp.concatenate([gate, push, slope_f * ps_f, slope_l * ps_l], 0).astype(BF16)
        yy[j] = jnp.concatenate(
            [
                silu_of(back_f, sig_bf),
                silu_of(za_f, sig_f),
                slope_f * ta_f,
                slope_l * ta_l,
                silu_of(back_l, sig_bl),
                silu_of(za_l, sig_l),
            ],
            0,
        ).astype(BF16)
        keep[j] = jnp.concatenate(
            [
                slope_of(back_l, sig_bl),
                slope_l,
                curve_of(za_l, sig_l) * ps_l * ta_l,
                slope_of(tan_l, logistic(tan_l)),
            ],
            0,
        )

    each_block(blocks, raise_all)

    def push_back(source):
        def body(j):
            chain2[j + 1] = dot_t(source[j, pl.ds(0, 16)], wu[j]) + chain2[links[1, j]]

        each_block(blocks, body)

    def settle(source, put):
        def body(b):
            put(b, (source[b, pl.ds(0, 16)].astype(F32) + chain2[links[3, b]]).astype(BF16))

        each_block(blocks, body)

    def lower(hidden, source, put):
        def body(i):
            put(i, (source[i].astype(F32) + dot(hidden[down_index[0, i]], wd[i])).astype(BF16))

        each_block(blocks, body)

    def in_block(ref):
        def put(i, value):
            ref[i] = value

        return put

    def in_rows(ref):
        def put(i, value):
            ref[:, cols(i)] = value

        return put

    def relay(kind, source, landing, to):
        copy = pltpu.make_async_remote_copy(
            src_ref=source,
            dst_ref=landing,
            send_sem=link_send.at[kind],
            recv_sem=link_recv.at[kind],
            device_id={"section": to},
            device_id_type=MESH,
        )
        copy.start()
        return copy

    push_back(e0)
    settle(cs, in_block(g_sent))
    g_copy = relay(0, g_sent, g1, before)
    lower(h0, v0, in_block(v_sent))
    v_copy = relay(1, v_sent, v1, after)

    def gather_y(i):
        ys[i] = yy[down_index[0, i]]

    each_block(blocks, gather_y)
    spread(2, ys, lambda d: ry.at[d])
    spread(3, e0, lambda d: re.at[d, :, pl.ds(0, 32)])
    ry[me] = ys[pl.ds(me * kept, kept)]
    re[me, :, pl.ds(0, 32)] = e0[pl.ds(me * kept, kept)]

    g_copy.wait_recv()
    spread(4, g1, lambda d: rc.at[d, :, pl.ds(32, 16)])
    rc[me, :, pl.ds(32, 16)] = g1[pl.ds(me * kept, kept)]

    def pull_later(i):
        chain[i + 1, pl.ds(0, 16)] = dot_t(g1[i], wd[i]) + chain[links[0, i], pl.ds(0, 16)]

    each_block(blocks, pull_later)

    def gate_later(j):
        pulled = chain[links[2, j], pl.ds(0, 16)]
        kept_rows = keep[j]
        gate = kept_rows[0:8] * pulled[0:8]
        push = kept_rows[8:16] * pulled[8:16] + kept_rows[16:24]
        e1[j] = jnp.concatenate([gate, push], 0).astype(BF16)

    each_block(blocks, gate_later)
    spread(5, e1, lambda d: re.at[d, :, pl.ds(32, 16)])
    re[me, :, pl.ds(32, 16)] = e1[pl.ds(me * kept, kept)]

    push_back(e1)
    settle(g1, in_rows(g_last))
    g_end = relay(2, g_last, ga_out, before)

    v_copy.wait_recv()

    def raise_later(j):
        z = dot(v1[up_index[0, j]], wu[j])
        zv, zt = z[0:8], z[8:16]
        h1[j] = jnp.concatenate([silu_of(zv, logistic(zv)), keep[j, pl.ds(24, 8)] * zt], 0).astype(BF16)

    each_block(blocks, raise_later)
    lower(h1, v1, in_rows(v_last))
    v_end = relay(3, v_last, vt_out, after)

    for copy in sent:
        copy.wait_recv()

    def rows_of(ref, k):
        return ref[:, k].reshape(n_dp * 48, BLOCK)

    for k in range(kept):
        for half, (left, right) in enumerate(((rx, re), (ry, rc))):
            grad = lax.dot_general(
                rows_of(left, k), rows_of(right, k), (((0,), (0,)), ((), ())), preferred_element_type=F32
            )
            grads_out[half, k] = (grad * scale).astype(BF16)

    for copy in sent:
        copy.wait_send()
    g_copy.wait_send()
    v_copy.wait_send()
    g_end.wait()
    v_end.wait()


def hand_out(vt, ga, grads, values, score, tangent, adjoint, up, down):
    values[0] = vt[pl.ds(0, 8)]
    tangent[0] = vt[pl.ds(8, 8)]
    score[0] = ga[pl.ds(0, 8)]
    adjoint[0] = ga[pl.ds(8, 8)]
    up[0] = grads[0]
    down[0] = grads[1]


def chain_links(down_index, up_index):
    index = jnp.concatenate([down_index, up_index], 0)
    count = index.shape[1]
    spot = jnp.arange(count, dtype=jnp.int32)
    own = jnp.concatenate([index, jnp.broadcast_to(spot, index.shape)], 0)
    over = jnp.concatenate([index, index], 0)
    limit = jnp.where(jnp.arange(4)[:, None] < 2, spot[None], count)
    hit = (own[:, :, None] == over[:, None, :]) & (spot[None, None, :] < limit[:, :, None])
    return jnp.max(jnp.where(hit, spot[None, None, :] + 1, 0), axis=2).astype(jnp.int32)


def on_device(mesh_shape, *arrays):
    (w_up, up_index, w_down, down_index, tick_order, *rest) = arrays
    n_section, n_dp = mesh_shape["section"], mesh_shape["dp"]
    blocks = w_up.shape[1]
    rows, width = rest[0].shape[1:]
    kept = blocks // n_dp
    links = chain_links(down_index, up_index)
    smem = pl.BlockSpec(memory_space=pltpu.SMEM)
    anywhere = pl.BlockSpec(memory_space=pl.ANY)
    vmem = pl.BlockSpec(memory_space=pltpu.VMEM)

    def by_block(height, copies=1):
        return pltpu.VMEM((copies * blocks, height, BLOCK), BF16)

    vt, ga, grads = pl.pallas_call(
        functools.partial(tick_kernel, n_section, n_dp, blocks, 1.0 / (rows * n_dp)),
        out_shape=(
            jax.ShapeDtypeStruct((16, width), BF16),
            jax.ShapeDtypeStruct((16, width), BF16),
            jax.ShapeDtypeStruct((2, kept, BLOCK, BLOCK), BF16),
        ),
        in_specs=[smem] * 4 + [anywhere] * 11,
        out_specs=(anywhere, anywhere, vmem),
        scratch_shapes=[
            pltpu.VMEM((blocks, BLOCK, BLOCK), BF16),
            pltpu.VMEM((blocks, BLOCK, BLOCK), BF16),
            pltpu.VMEM((2, 32, width), BF16),
            pltpu.VMEM((16, width), BF16),
            pltpu.VMEM((32, width), BF16),
            by_block(32, 2),
            by_block(8, 2),
            by_block(32),
            by_block(48),
            by_block(32),
            *[by_block(16)] * 5,
            *[pltpu.VMEM((16, width), BF16)] * 2,
            by_block(48),
            by_block(48),
            by_block(32),
            *[by_block(16)] * 3,
            *[pltpu.VMEM((n_dp, kept, 48, BLOCK), BF16)] * 4,
            pltpu.VMEM((blocks + 1, 32, BLOCK), F32),
            pltpu.VMEM((blocks + 1, 16, BLOCK), F32),
            pltpu.VMEM((blocks, 32, BLOCK), F32),
            pltpu.SemaphoreType.DMA((16,)),
            pltpu.SemaphoreType.DMA((6, n_dp - 1)),
            pltpu.SemaphoreType.DMA((6, n_dp - 1)),
            pltpu.SemaphoreType.DMA((4,)),
            pltpu.SemaphoreType.DMA((4,)),
        ],
        compiler_params=pltpu.CompilerParams(
            collective_id=0, has_side_effects=True, vmem_limit_bytes=40 << 20
        ),
        name="ticks",
    )(up_index, down_index, tick_order, links, w_up, w_down, *rest)
    stream = jax.ShapeDtypeStruct((1, rows, width), BF16)
    grad = jax.ShapeDtypeStruct((1, kept, BLOCK, BLOCK), BF16)
    return pl.pallas_call(
        hand_out,
        out_shape=(stream,) * 4 + (grad,) * 2,
        in_specs=[vmem] * 3,
        out_specs=(vmem,) * 6,
        name="hand_out",
    )(vt, ga, grads)


def solution(mesh):
    matrix = P("section", None, None, None)
    table = P("section", None)
    stream = P("section", "dp", None)
    saved = P("section", None, "dp", None)
    return jax.shard_map(
        functools.partial(on_device, dict(mesh.shape)),
        mesh=mesh,
        in_specs=(matrix, table, matrix, table, table) + (stream,) * 4 + (saved,) * 5,
        out_specs=(stream,) * 4 + (P("section", "dp", None, None),) * 2,
        check_vma=False,
    )
```

```python
import functools

import jax
import jax.numpy as jnp
from jax import lax
from jax.experimental import pallas as pl
from jax.experimental.pallas import tpu as pltpu
from jax.sharding import PartitionSpec as P

BLOCK = 128
UNROLL = 8
MESH = pl.DeviceIdType.MESH
F32 = jnp.float32
BF16 = jnp.bfloat16


def logistic(z):
    return 0.5 * jnp.tanh(0.5 * z) + 0.5


def silu_of(z, sig):
    return z * sig


def slope_of(z, sig):
    return sig * (1.0 + z * (1.0 - sig))


def curve_of(z, sig):
    return sig * (1.0 - sig) * (2.0 + z * (1.0 - 2.0 * sig))


def cols(i, width=BLOCK):
    return pl.ds(pl.multiple_of(i * width, width), width)


def each_block(count, body):
    def step(t, carry):
        for u in range(UNROLL):
            body(t * UNROLL + u)
        return carry

    lax.fori_loop(0, count // UNROLL, step, 0)


def dot(a, b):
    return jnp.dot(a, b, preferred_element_type=F32)


def dot_t(a, b):
    return lax.dot_general(a, b, (((1,), (1,)), ((), ())), preferred_element_type=F32)


def tick_kernel(
    n_section, n_dp, blocks, scale,
    up_index, down_index, tick_order, links,
    w_up, w_down, values_in, score_in, tangent_in, adjoint_in,
    saved_back, saved_tan, saved_second, saved_second_tan, saved_second_grad,
    v_out, g_out, grads_out,
    wu, wd, raw_x, raw_v, raw_c, x_slots, c_slots, xt, xs, cs,
    v0, v1, g1, v_sent, g_sent, v_last, g_last, grads,
    ys, yy, e0, e1, h0, h1, rx, ry, rc, re,
    chain, chain2, keep,
    in_sem, send_sem, recv_sem, link_send, link_recv,
):
    section = lax.axis_index("section")
    me = lax.axis_index("dp")
    after = lax.rem(section + 1, n_section)
    before = lax.rem(section + n_section - 1, n_section)
    kept = blocks // n_dp

    loads = []

    def load(source, target):
        copy = pltpu.make_async_copy(source, target, in_sem.at[len(loads)])
        copy.start()
        loads.append(copy)

    for slot in range(2):
        for at, saved in enumerate((saved_back, saved_second, saved_second_tan, saved_tan)):
            load(saved.at[0, slot], raw_x.at[slot, pl.ds(8 * at, 8)])
    load(score_in.at[0], raw_c.at[pl.ds(0, 8)])
    load(adjoint_in.at[0], raw_c.at[pl.ds(8, 8)])
    for slot in range(2):
        load(saved_second_grad.at[0, slot], raw_c.at[pl.ds(16 + 8 * slot, 8)])
    early = len(loads)
    load(values_in.at[0], raw_v.at[pl.ds(0, 8)])
    load(tangent_in.at[0], raw_v.at[pl.ds(8, 8)])
    load(w_down.at[0], wd)
    load(w_up.at[0], wu)

    barrier = pltpu.get_barrier_semaphore()
    for p in range(1, n_dp):
        pl.semaphore_signal(barrier, inc=1, device_id={"dp": lax.rem(me + p, n_dp)}, device_id_type=MESH)
    for s in (after, before):
        pl.semaphore_signal(barrier, inc=1, device_id={"section": s}, device_id_type=MESH)

    first = tick_order[0, 0] * blocks
    later = tick_order[0, 1] * blocks

    chain[0] = jnp.zeros(chain.shape[1:], F32)
    chain2[0] = jnp.zeros(chain2.shape[1:], F32)

    for copy in loads[:early]:
        copy.wait()

    def to_blocks(j):
        here = cols(j)
        for slot in range(2):
            x_slots[slot * blocks + j] = raw_x[slot, :, here]
            c_slots[slot * blocks + j] = raw_c[pl.ds(16 + 8 * slot, 8), here]
        cs[j, pl.ds(0, 16)] = raw_c[pl.ds(0, 16), here]

    each_block(blocks, to_blocks)

    def gather_x(j):
        source = up_index[0, j]
        xs[j, pl.ds(0, 24)] = x_slots[first + source, pl.ds(0, 24)]
        xs[j, pl.ds(24, 8)] = x_slots[later + source, pl.ds(16, 8)]
        xs[j, pl.ds(32, 16)] = x_slots[later + source, pl.ds(0, 16)]
        cs[j, pl.ds(16, 8)] = c_slots[first + j]
        cs[j, pl.ds(24, 8)] = c_slots[later + j]

    each_block(blocks, gather_x)
    pl.semaphore_wait(barrier, n_dp + 1)

    sent = []

    def slab(ref, d):
        return ref.at[pl.ds(d * kept, kept)]

    def spread(kind, source, landing):
        for p in range(1, n_dp):
            peer = lax.rem(me + p, n_dp)
            copy = pltpu.make_async_remote_copy(
                src_ref=slab(source, peer),
                dst_ref=landing(me),
                send_sem=send_sem.at[kind, p - 1],
                recv_sem=recv_sem.at[kind, p - 1],
                device_id={"dp": peer},
                device_id_type=MESH,
            )
            copy.start()
            sent.append(copy)

    spread(0, xs, lambda d: rx.at[d])
    spread(1, cs, lambda d: rc.at[d, :, pl.ds(0, 32)])
    rx[me] = xs[pl.ds(me * kept, kept)]
    rc[me, :, pl.ds(0, 32)] = cs[pl.ds(me * kept, kept)]

    for copy in loads[early : early + 2]:
        copy.wait()

    def to_blocks_v(j):
        v0[j] = raw_v[:, cols(j)]

    each_block(blocks, to_blocks_v)

    def gather_v(j):
        source = up_index[0, j]
        xt[j, pl.ds(0, 16)] = v0[source]
        xt[j, pl.ds(16, 8)] = x_slots[first + source, pl.ds(24, 8)]
        xt[j, pl.ds(24, 8)] = x_slots[later + source, pl.ds(24, 8)]

    each_block(blocks, gather_v)
    loads[early + 2].wait()

    def pull(i):
        chain[i + 1] = dot_t(cs[i], wd[i]) + chain[links[0, i]]

    each_block(blocks, pull)
    loads[early + 3].wait()

    def raise_all(j):
        z = dot(jnp.concatenate([xt[j], xs[j]], 0), wu[j])
        zv, zt, tan_f, tan_l = z[0:8], z[8:16], z[16:24], z[24:32]
        back_f, za_f, ta_f = z[32:40], z[40:48], z[48:56]
        ta_l, back_l, za_l = z[56:64], z[64:72], z[72:80]
        pulled = chain[links[2, j]]
        pg, pa, ps_f, ps_l = pulled[0:8], pulled[8:16], pulled[16:24], pulled[24:32]
        sig_f, sig_l = logistic(za_f), logistic(za_l)
        slope_f, slope_l = slope_of(za_f, sig_f), slope_of(za_l, sig_l)
        sig_bf, sig_bl = logistic(back_f), logistic(back_l)
        hidden = silu_of(zv, logistic(zv))
        tangent_hidden = slope_of(tan_f, logistic(tan_f)) * zt
        h0[j] = jnp.concatenate([hidden, tangent_hidden], 0).astype(BF16)
        gate = slope_of(back_f, sig_bf) * pg
        push = slope_f * pa + curve_of(za_f, sig_f) * ps_f * ta_f
        e0[j] = jnp.concatenate([gate, push, slope_f * ps_f, slope_l * ps_l], 0).astype(BF16)
        yy[j] = jnp.concatenate(
            [
                silu_of(back_f, sig_bf),
                silu_of(za_f, sig_f),
                slope_f * ta_f,
                slope_l * ta_l,
                silu_of(back_l, sig_bl),
                silu_of(za_l, sig_l),
            ],
            0,
        ).astype(BF16)
        keep[j] = jnp.concatenate(
            [
                slope_of(back_l, sig_bl),
                slope_l,
                curve_of(za_l, sig_l) * ps_l * ta_l,
                slope_of(tan_l, logistic(tan_l)),
            ],
            0,
        )

    each_block(blocks, raise_all)

    def push_back(source):
        def body(j):
            chain2[j + 1] = dot_t(source[j, pl.ds(0, 16)], wu[j]) + chain2[links[1, j]]

        each_block(blocks, body)

    def settle(source, put):
        def body(b):
            put(b, (source[b, pl.ds(0, 16)].astype(F32) + chain2[links[3, b]]).astype(BF16))

        each_block(blocks, body)

    def lower(hidden, source, put):
        def body(i):
            put(i, (source[i].astype(F32) + dot(hidden[down_index[0, i]], wd[i])).astype(BF16))

        each_block(blocks, body)

    def in_block(ref):
        def put(i, value):
            ref[i] = value

        return put

    def in_rows(ref):
        def put(i, value):
            ref[0, :, cols(i)] = value[0:8]
            ref[1, :, cols(i)] = value[8:16]

        return put

    def relay(kind, source, landing, to):
        copy = pltpu.make_async_remote_copy(
            src_ref=source,
            dst_ref=landing,
            send_sem=link_send.at[kind],
            recv_sem=link_recv.at[kind],
            device_id={"section": to},
            device_id_type=MESH,
        )
        copy.start()
        return copy

    push_back(e0)
    settle(cs, in_block(g_sent))
    g_copy = relay(0, g_sent, g1, before)
    lower(h0, v0, in_block(v_sent))
    v_copy = relay(1, v_sent, v1, after)

    def gather_y(i):
        ys[i] = yy[down_index[0, i]]

    each_block(blocks, gather_y)
    spread(2, ys, lambda d: ry.at[d])
    spread(3, e0, lambda d: re.at[d, :, pl.ds(0, 32)])
    ry[me] = ys[pl.ds(me * kept, kept)]
    re[me, :, pl.ds(0, 32)] = e0[pl.ds(me * kept, kept)]

    g_copy.wait_recv()
    spread(4, g1, lambda d: rc.at[d, :, pl.ds(32, 16)])
    rc[me, :, pl.ds(32, 16)] = g1[pl.ds(me * kept, kept)]

    def pull_later(i):
        chain[i + 1, pl.ds(0, 16)] = dot_t(g1[i], wd[i]) + chain[links[0, i], pl.ds(0, 16)]

    each_block(blocks, pull_later)

    def gate_later(j):
        pulled = chain[links[2, j], pl.ds(0, 16)]
        kept_rows = keep[j]
        gate = kept_rows[0:8] * pulled[0:8]
        push = kept_rows[8:16] * pulled[8:16] + kept_rows[16:24]
        e1[j] = jnp.concatenate([gate, push], 0).astype(BF16)

    each_block(blocks, gate_later)
    spread(5, e1, lambda d: re.at[d, :, pl.ds(32, 16)])
    re[me, :, pl.ds(32, 16)] = e1[pl.ds(me * kept, kept)]

    push_back(e1)
    settle(g1, in_rows(g_last))
    g_end = relay(2, g_last, g_out, before)

    v_copy.wait_recv()

    def raise_later(j):
        z = dot(v1[up_index[0, j]], wu[j])
        zv, zt = z[0:8], z[8:16]
        h1[j] = jnp.concatenate([silu_of(zv, logistic(zv)), keep[j, pl.ds(24, 8)] * zt], 0).astype(BF16)

    each_block(blocks, raise_later)
    lower(h1, v1, in_rows(v_last))
    v_end = relay(3, v_last, v_out, after)

    for copy in sent:
        copy.wait_recv()

    def rows_of(ref, k):
        return ref[:, k].reshape(n_dp * 48, BLOCK)

    for k in range(kept):
        for half, (left, right) in enumerate(((rx, re), (ry, rc))):
            grad = lax.dot_general(
                rows_of(left, k), rows_of(right, k), (((0,), (0,)), ((), ())), preferred_element_type=F32
            )
            grads[half, k] = (grad * scale).astype(BF16)

    grad_copy = pltpu.make_async_copy(grads, grads_out, in_sem.at[len(loads)])
    grad_copy.start()
    for copy in sent:
        copy.wait_send()
    grad_copy.wait()
    g_copy.wait_send()
    v_copy.wait_send()
    g_end.wait()
    v_end.wait()


def hand_out(v, g, grads, values, score, tangent, adjoint, up, down, sem):
    moves = ((v, 0, values), (v, 1, tangent), (g, 0, score), (g, 1, adjoint), (grads, 0, up), (grads, 1, down))
    copies = [
        pltpu.make_async_copy(source.at[half], target.at[0], sem.at[n])
        for n, (source, half, target) in enumerate(moves)
    ]
    for copy in copies:
        copy.start()
    for copy in copies:
        copy.wait()


def chain_links(down_index, up_index):
    index = jnp.concatenate([down_index, up_index], 0)
    count = index.shape[1]
    spot = jnp.arange(count, dtype=jnp.int32)
    own = jnp.concatenate([index, jnp.broadcast_to(spot, index.shape)], 0)
    over = jnp.concatenate([index, index], 0)
    limit = jnp.where(jnp.arange(4)[:, None] < 2, spot[None], count)
    hit = (own[:, :, None] == over[:, None, :]) & (spot[None, None, :] < limit[:, :, None])
    return jnp.max(jnp.where(hit, spot[None, None, :] + 1, 0), axis=2).astype(jnp.int32)


def on_device(mesh_shape, *arrays):
    (w_up, up_index, w_down, down_index, tick_order, *rest) = arrays
    n_section, n_dp = mesh_shape["section"], mesh_shape["dp"]
    blocks = w_up.shape[1]
    rows, width = rest[0].shape[1:]
    kept = blocks // n_dp
    links = chain_links(down_index, up_index)
    smem = pl.BlockSpec(memory_space=pltpu.SMEM)
    hbm = pl.BlockSpec(memory_space=pltpu.HBM)

    def by_block(height, copies=1):
        return pltpu.VMEM((copies * blocks, height, BLOCK), BF16)

    v, g, grads = pl.pallas_call(
        functools.partial(tick_kernel, n_section, n_dp, blocks, 1.0 / (rows * n_dp)),
        out_shape=(
            jax.ShapeDtypeStruct((2, rows, width), BF16),
            jax.ShapeDtypeStruct((2, rows, width), BF16),
            jax.ShapeDtypeStruct((2, kept, BLOCK, BLOCK), BF16),
        ),
        in_specs=[smem] * 4 + [hbm] * 11,
        out_specs=(hbm, hbm, hbm),
        scratch_shapes=[
            pltpu.VMEM((blocks, BLOCK, BLOCK), BF16),
            pltpu.VMEM((blocks, BLOCK, BLOCK), BF16),
            pltpu.VMEM((2, 32, width), BF16),
            pltpu.VMEM((16, width), BF16),
            pltpu.VMEM((32, width), BF16),
            by_block(32, 2),
            by_block(8, 2),
            by_block(32),
            by_block(48),
            by_block(32),
            *[by_block(16)] * 5,
            *[pltpu.VMEM((2, 8, width), BF16)] * 2,
            pltpu.VMEM((2, kept, BLOCK, BLOCK), BF16),
            by_block(48),
            by_block(48),
            by_block(32),
            *[by_block(16)] * 3,
            *[pltpu.VMEM((n_dp, kept, 48, BLOCK), BF16)] * 4,
            pltpu.VMEM((blocks + 1, 32, BLOCK), F32),
            pltpu.VMEM((blocks + 1, 16, BLOCK), F32),
            pltpu.VMEM((blocks, 32, BLOCK), F32),
            pltpu.SemaphoreType.DMA((17,)),
            pltpu.SemaphoreType.DMA((6, n_dp - 1)),
            pltpu.SemaphoreType.DMA((6, n_dp - 1)),
            pltpu.SemaphoreType.DMA((4,)),
            pltpu.SemaphoreType.DMA((4,)),
        ],
        compiler_params=pltpu.CompilerParams(
            collective_id=0, has_side_effects=True, vmem_limit_bytes=56 << 20
        ),
        name="ticks",
    )(up_index, down_index, tick_order, links, w_up, w_down, *rest)
    stream = jax.ShapeDtypeStruct((1, rows, width), BF16)
    grad = jax.ShapeDtypeStruct((1, kept, BLOCK, BLOCK), BF16)
    return pl.pallas_call(
        hand_out,
        out_shape=(stream,) * 4 + (grad,) * 2,
        in_specs=[hbm] * 3,
        out_specs=(hbm,) * 6,
        scratch_shapes=[pltpu.SemaphoreType.DMA((6,))],
        name="hand_out",
    )(v, g, grads)


def solution(mesh):
    matrix = P("section", None, None, None)
    table = P("section", None)
    stream = P("section", "dp", None)
    saved = P("section", None, "dp", None)
    return jax.shard_map(
        functools.partial(on_device, dict(mesh.shape)),
        mesh=mesh,
        in_specs=(matrix, table, matrix, table, table) + (stream,) * 4 + (saved,) * 5,
        out_specs=(stream,) * 4 + (P("section", "dp", None, None),) * 2,
        check_vma=False,
    )
```

```python
import functools

import jax
import jax.numpy as jnp
from jax import lax
from jax.experimental import pallas as pl
from jax.experimental.pallas import tpu as pltpu
from jax.sharding import PartitionSpec as P

BLOCK = 128
UNROLL = 8
MESH = pl.DeviceIdType.MESH
F32 = jnp.float32
BF16 = jnp.bfloat16


def logistic(z):
    return 0.5 * jnp.tanh(0.5 * z) + 0.5


def silu_of(z, sig):
    return z * sig


def slope_of(z, sig):
    return sig * (1.0 + z * (1.0 - sig))


def curve_of(z, sig):
    return sig * (1.0 - sig) * (2.0 + z * (1.0 - 2.0 * sig))


def cols(i, width=BLOCK):
    return pl.ds(pl.multiple_of(i * width, width), width)


def each_block(count, body):
    def step(t, carry):
        for u in range(UNROLL):
            body(t * UNROLL + u)
        return carry

    lax.fori_loop(0, count // UNROLL, step, 0)


def dot(a, b):
    return jnp.dot(a, b, preferred_element_type=F32)


def dot_t(a, b):
    return lax.dot_general(a, b, (((1,), (1,)), ((), ())), preferred_element_type=F32)


def tick_kernel(
    n_section, n_dp, blocks, scale,
    up_index, down_index, tick_order, links,
    w_up, w_down, values_in, score_in, tangent_in, adjoint_in,
    saved_back, saved_tan, saved_second, saved_second_tan, saved_second_grad,
    v_out, g_out, grads_out,
    wu, wd, raw_x, raw_v, raw_c, x_slots, c_slots, xt, xs, cs,
    v0, v1, g1, v_sent, g_sent, v_last, g_last, grads,
    ys, yy, e0, e1, h0, h1, rx, ry, rc, re,
    chain, chain2, keep,
    in_sem, send_sem, recv_sem, link_send, link_recv,
):
    section = lax.axis_index("section")
    me = lax.axis_index("dp")
    after = lax.rem(section + 1, n_section)
    before = lax.rem(section + n_section - 1, n_section)
    kept = blocks // n_dp

    loads = []

    def load(source, target):
        copy = pltpu.make_async_copy(source, target, in_sem.at[len(loads)])
        copy.start()
        loads.append(copy)

    for slot in range(2):
        for at, saved in enumerate((saved_back, saved_second, saved_second_tan, saved_tan)):
            load(saved.at[0, slot], raw_x.at[slot, pl.ds(8 * at, 8)])
    load(score_in.at[0], raw_c.at[pl.ds(0, 8)])
    load(adjoint_in.at[0], raw_c.at[pl.ds(8, 8)])
    for slot in range(2):
        load(saved_second_grad.at[0, slot], raw_c.at[pl.ds(16 + 8 * slot, 8)])
    early = len(loads)
    load(values_in.at[0], raw_v.at[pl.ds(0, 8)])
    load(tangent_in.at[0], raw_v.at[pl.ds(8, 8)])
    load(w_down.at[0], wd)
    load(w_up.at[0], wu)

    barrier = pltpu.get_barrier_semaphore()
    for p in range(1, n_dp):
        pl.semaphore_signal(barrier, inc=1, device_id={"dp": lax.rem(me + p, n_dp)}, device_id_type=MESH)
    for s in (after, before):
        pl.semaphore_signal(barrier, inc=1, device_id={"section": s}, device_id_type=MESH)

    first = tick_order[0, 0] * blocks
    later = tick_order[0, 1] * blocks

    chain[0] = jnp.zeros(chain.shape[1:], F32)
    chain2[0] = jnp.zeros(chain2.shape[1:], F32)

    for copy in loads[:early]:
        copy.wait()

    def to_blocks(j):
        here = cols(j)
        for slot in range(2):
            x_slots[slot * blocks + j] = raw_x[slot, :, here]
            c_slots[slot * blocks + j] = raw_c[pl.ds(16 + 8 * slot, 8), here]
        cs[j, pl.ds(0, 16)] = raw_c[pl.ds(0, 16), here]

    each_block(blocks, to_blocks)

    def gather_x(j):
        source = up_index[0, j]
        xs[j, pl.ds(0, 24)] = x_slots[first + source, pl.ds(0, 24)]
        xs[j, pl.ds(24, 8)] = x_slots[later + source, pl.ds(16, 8)]
        xs[j, pl.ds(32, 16)] = x_slots[later + source, pl.ds(0, 16)]
        cs[j, pl.ds(16, 8)] = c_slots[first + j]
        cs[j, pl.ds(24, 8)] = c_slots[later + j]

    each_block(blocks, gather_x)
    pl.semaphore_wait(barrier, n_dp + 1)

    sent = []

    def slab(ref, d):
        return ref.at[pl.ds(d * kept, kept)]

    def spread(kind, source, landing):
        for p in range(1, n_dp):
            peer = lax.rem(me + p, n_dp)
            copy = pltpu.make_async_remote_copy(
                src_ref=slab(source, peer),
                dst_ref=landing(me),
                send_sem=send_sem.at[kind, p - 1],
                recv_sem=recv_sem.at[kind, p - 1],
                device_id={"dp": peer},
                device_id_type=MESH,
            )
            copy.start()
            sent.append(copy)

    spread(0, xs, lambda d: rx.at[d])
    spread(1, cs, lambda d: rc.at[d, :, pl.ds(0, 32)])
    rx[me] = xs[pl.ds(me * kept, kept)]
    rc[me, :, pl.ds(0, 32)] = cs[pl.ds(me * kept, kept)]

    for copy in loads[early : early + 2]:
        copy.wait()

    def to_blocks_v(j):
        v0[j] = raw_v[:, cols(j)]

    each_block(blocks, to_blocks_v)

    def gather_v(j):
        source = up_index[0, j]
        xt[j, pl.ds(0, 16)] = v0[source]
        xt[j, pl.ds(16, 8)] = x_slots[first + source, pl.ds(24, 8)]
        xt[j, pl.ds(24, 8)] = x_slots[later + source, pl.ds(24, 8)]

    each_block(blocks, gather_v)
    loads[early + 2].wait()

    def pull(i):
        chain[i + 1] = dot_t(cs[i], wd[i]) + chain[links[0, i]]

    each_block(blocks, pull)
    loads[early + 3].wait()

    def raise_all(j):
        z = dot(jnp.concatenate([xt[j], xs[j]], 0), wu[j])
        zv, zt, tan_f, tan_l = z[0:8], z[8:16], z[16:24], z[24:32]
        back_f, za_f, ta_f = z[32:40], z[40:48], z[48:56]
        ta_l, back_l, za_l = z[56:64], z[64:72], z[72:80]
        pulled = chain[links[2, j]]
        pg, pa, ps_f, ps_l = pulled[0:8], pulled[8:16], pulled[16:24], pulled[24:32]
        sig_f, sig_l = logistic(za_f), logistic(za_l)
        slope_f, slope_l = slope_of(za_f, sig_f), slope_of(za_l, sig_l)
        sig_bf, sig_bl = logistic(back_f), logistic(back_l)
        hidden = silu_of(zv, logistic(zv))
        tangent_hidden = slope_of(tan_f, logistic(tan_f)) * zt
        h0[j] = jnp.concatenate([hidden, tangent_hidden], 0).astype(BF16)
        gate = slope_of(back_f, sig_bf) * pg
        push = slope_f * pa + curve_of(za_f, sig_f) * ps_f * ta_f
        e0[j] = jnp.concatenate([gate, push, slope_f * ps_f, slope_l * ps_l], 0).astype(BF16)
        yy[j] = jnp.concatenate(
            [
                silu_of(back_f, sig_bf),
                silu_of(za_f, sig_f),
                slope_f * ta_f,
                slope_l * ta_l,
                silu_of(back_l, sig_bl),
                silu_of(za_l, sig_l),
            ],
            0,
        ).astype(BF16)
        keep[j] = jnp.concatenate(
            [
                slope_of(back_l, sig_bl),
                slope_l,
                curve_of(za_l, sig_l) * ps_l * ta_l,
                slope_of(tan_l, logistic(tan_l)),
            ],
            0,
        )

    each_block(blocks, raise_all)

    def push_back(source):
        def body(j):
            chain2[j + 1] = dot_t(source[j, pl.ds(0, 16)], wu[j]) + chain2[links[1, j]]

        each_block(blocks, body)

    def settle(source, put):
        def body(b):
            put(b, (source[b, pl.ds(0, 16)].astype(F32) + chain2[links[3, b]]).astype(BF16))

        each_block(blocks, body)

    def lower(hidden, source, put):
        def body(i):
            put(i, (source[i].astype(F32) + dot(hidden[down_index[0, i]], wd[i])).astype(BF16))

        each_block(blocks, body)

    def in_block(ref):
        def put(i, value):
            ref[i] = value

        return put

    def in_rows(ref):
        def put(i, value):
            ref[0, :, cols(i)] = value[0:8]
            ref[1, :, cols(i)] = value[8:16]

        return put

    def relay(kind, source, landing, to):
        copy = pltpu.make_async_remote_copy(
            src_ref=source,
            dst_ref=landing,
            send_sem=link_send.at[kind],
            recv_sem=link_recv.at[kind],
            device_id={"section": to},
            device_id_type=MESH,
        )
        copy.start()
        return copy

    push_back(e0)
    settle(cs, in_block(g_sent))
    g_copy = relay(0, g_sent, g1, before)
    lower(h0, v0, in_block(v_sent))
    v_copy = relay(1, v_sent, v1, after)

    def gather_y(i):
        ys[i] = yy[down_index[0, i]]

    each_block(blocks, gather_y)
    spread(2, ys, lambda d: ry.at[d])
    spread(3, e0, lambda d: re.at[d, :, pl.ds(0, 32)])
    ry[me] = ys[pl.ds(me * kept, kept)]
    re[me, :, pl.ds(0, 32)] = e0[pl.ds(me * kept, kept)]

    g_copy.wait_recv()
    spread(4, g1, lambda d: rc.at[d, :, pl.ds(32, 16)])
    rc[me, :, pl.ds(32, 16)] = g1[pl.ds(me * kept, kept)]

    def pull_later(i):
        chain[i + 1, pl.ds(0, 16)] = dot_t(g1[i], wd[i]) + chain[links[0, i], pl.ds(0, 16)]

    each_block(blocks, pull_later)

    def gate_later(j):
        pulled = chain[links[2, j], pl.ds(0, 16)]
        kept_rows = keep[j]
        gate = kept_rows[0:8] * pulled[0:8]
        push = kept_rows[8:16] * pulled[8:16] + kept_rows[16:24]
        e1[j] = jnp.concatenate([gate, push], 0).astype(BF16)

    each_block(blocks, gate_later)
    spread(5, e1, lambda d: re.at[d, :, pl.ds(32, 16)])
    re[me, :, pl.ds(32, 16)] = e1[pl.ds(me * kept, kept)]

    push_back(e1)
    settle(g1, in_rows(g_last))
    g_end = relay(2, g_last, g_out, before)

    v_copy.wait_recv()

    def raise_later(j):
        z = dot(v1[up_index[0, j]], wu[j])
        zv, zt = z[0:8], z[8:16]
        h1[j] = jnp.concatenate([silu_of(zv, logistic(zv)), keep[j, pl.ds(24, 8)] * zt], 0).astype(BF16)

    each_block(blocks, raise_later)
    lower(h1, v1, in_rows(v_last))
    v_end = relay(3, v_last, v_out, after)

    for copy in sent:
        copy.wait_recv()

    def rows_of(ref, k):
        return ref[:, k].reshape(n_dp * 48, BLOCK)

    for k in range(kept):
        for half, (left, right) in enumerate(((rx, re), (ry, rc))):
            grad = lax.dot_general(
                rows_of(left, k), rows_of(right, k), (((0,), (0,)), ((), ())), preferred_element_type=F32
            )
            grads[half, k] = (grad * scale).astype(BF16)

    grad_copy = pltpu.make_async_copy(grads, grads_out, in_sem.at[len(loads)])
    grad_copy.start()
    for copy in sent:
        copy.wait_send()
    grad_copy.wait()
    g_copy.wait_send()
    v_copy.wait_send()
    g_end.wait()
    v_end.wait()


def hand_out(v, g, grads, values, score, tangent, adjoint, up, down, held, held_grads, in_sem, out_sem):
    moves = (
        (v, 0, values, held.at[0]),
        (v, 1, tangent, held.at[1]),
        (g, 0, score, held.at[2]),
        (g, 1, adjoint, held.at[3]),
        (grads, 0, up, held_grads.at[0]),
        (grads, 1, down, held_grads.at[1]),
    )
    inward = [
        pltpu.make_async_copy(source.at[half], stop, in_sem.at[n]) for n, (source, half, _, stop) in enumerate(moves)
    ]
    outward = [pltpu.make_async_copy(stop, target.at[0], out_sem.at[n]) for n, (_, _, target, stop) in enumerate(moves)]
    for copy in inward:
        copy.start()
    for arrived, copy in zip(inward, outward):
        arrived.wait()
        copy.start()
    for copy in outward:
        copy.wait()


def chain_links(down_index, up_index):
    index = jnp.concatenate([down_index, up_index], 0)
    count = index.shape[1]
    spot = jnp.arange(count, dtype=jnp.int32)
    own = jnp.concatenate([index, jnp.broadcast_to(spot, index.shape)], 0)
    over = jnp.concatenate([index, index], 0)
    limit = jnp.where(jnp.arange(4)[:, None] < 2, spot[None], count)
    hit = (own[:, :, None] == over[:, None, :]) & (spot[None, None, :] < limit[:, :, None])
    return jnp.max(jnp.where(hit, spot[None, None, :] + 1, 0), axis=2).astype(jnp.int32)


def on_device(mesh_shape, *arrays):
    (w_up, up_index, w_down, down_index, tick_order, *rest) = arrays
    n_section, n_dp = mesh_shape["section"], mesh_shape["dp"]
    blocks = w_up.shape[1]
    rows, width = rest[0].shape[1:]
    kept = blocks // n_dp
    links = chain_links(down_index, up_index)
    smem = pl.BlockSpec(memory_space=pltpu.SMEM)
    hbm = pl.BlockSpec(memory_space=pltpu.HBM)

    def by_block(height, copies=1):
        return pltpu.VMEM((copies * blocks, height, BLOCK), BF16)

    v, g, grads = pl.pallas_call(
        functools.partial(tick_kernel, n_section, n_dp, blocks, 1.0 / (rows * n_dp)),
        out_shape=(
            jax.ShapeDtypeStruct((2, rows, width), BF16),
            jax.ShapeDtypeStruct((2, rows, width), BF16),
            jax.ShapeDtypeStruct((2, kept, BLOCK, BLOCK), BF16),
        ),
        in_specs=[smem] * 4 + [hbm] * 11,
        out_specs=(hbm, hbm, hbm),
        scratch_shapes=[
            pltpu.VMEM((blocks, BLOCK, BLOCK), BF16),
            pltpu.VMEM((blocks, BLOCK, BLOCK), BF16),
            pltpu.VMEM((2, 32, width), BF16),
            pltpu.VMEM((16, width), BF16),
            pltpu.VMEM((32, width), BF16),
            by_block(32, 2),
            by_block(8, 2),
            by_block(32),
            by_block(48),
            by_block(32),
            *[by_block(16)] * 5,
            *[pltpu.VMEM((2, 8, width), BF16)] * 2,
            pltpu.VMEM((2, kept, BLOCK, BLOCK), BF16),
            by_block(48),
            by_block(48),
            by_block(32),
            *[by_block(16)] * 3,
            *[pltpu.VMEM((n_dp, kept, 48, BLOCK), BF16)] * 4,
            pltpu.VMEM((blocks + 1, 32, BLOCK), F32),
            pltpu.VMEM((blocks + 1, 16, BLOCK), F32),
            pltpu.VMEM((blocks, 32, BLOCK), F32),
            pltpu.SemaphoreType.DMA((17,)),
            pltpu.SemaphoreType.DMA((6, n_dp - 1)),
            pltpu.SemaphoreType.DMA((6, n_dp - 1)),
            pltpu.SemaphoreType.DMA((4,)),
            pltpu.SemaphoreType.DMA((4,)),
        ],
        compiler_params=pltpu.CompilerParams(
            collective_id=0, has_side_effects=True, vmem_limit_bytes=56 << 20
        ),
        name="ticks",
    )(up_index, down_index, tick_order, links, w_up, w_down, *rest)
    stream = jax.ShapeDtypeStruct((1, rows, width), BF16)
    grad = jax.ShapeDtypeStruct((1, kept, BLOCK, BLOCK), BF16)
    return pl.pallas_call(
        hand_out,
        out_shape=(stream,) * 4 + (grad,) * 2,
        in_specs=[hbm] * 3,
        out_specs=(hbm,) * 6,
        scratch_shapes=[
            pltpu.VMEM((4, rows, width), BF16),
            pltpu.VMEM((2, kept, BLOCK, BLOCK), BF16),
            pltpu.SemaphoreType.DMA((6,)),
            pltpu.SemaphoreType.DMA((6,)),
        ],
        compiler_params=pltpu.CompilerParams(vmem_limit_bytes=56 << 20),
        name="hand_out",
    )(v, g, grads)


def solution(mesh):
    matrix = P("section", None, None, None)
    table = P("section", None)
    stream = P("section", "dp", None)
    saved = P("section", None, "dp", None)
    return jax.shard_map(
        functools.partial(on_device, dict(mesh.shape)),
        mesh=mesh,
        in_specs=(matrix, table, matrix, table, table) + (stream,) * 4 + (saved,) * 5,
        out_specs=(stream,) * 4 + (P("section", "dp", None, None),) * 2,
        check_vma=False,
    )
```

```python
import functools

import jax
import jax.numpy as jnp
from jax import lax
from jax.experimental import pallas as pl
from jax.experimental.pallas import tpu as pltpu
from jax.sharding import PartitionSpec as P

BLOCK = 128
UNROLL = 32
ALONG_X = (2, 1, 3)
FAR_FIRST = ((2, 1), (2, 0), (1, 1), (1, 0), (3, 1), (3, 0), (0, 1))
MESH = pl.DeviceIdType.MESH
F32 = jnp.float32
BF16 = jnp.bfloat16


def logistic(z):
    return 0.5 * jnp.tanh(0.5 * z) + 0.5


def silu_of(z, sig):
    return z * sig


def slope_of(z, sig):
    return sig * (1.0 + z * (1.0 - sig))


def curve_of(z, sig):
    return sig * (1.0 - sig) * (2.0 + z * (1.0 - 2.0 * sig))


def cols(i, width=BLOCK):
    return pl.ds(pl.multiple_of(i * width, width), width)


def each_block(count, body):
    def step(i, carry):
        body(i)
        return carry

    lax.fori_loop(0, count, step, 0, unroll=UNROLL)


def dot(a, b):
    return jnp.dot(a, b, preferred_element_type=F32)


def dot_rows(a, b):
    return lax.dot_general(a, b, (((0,), (0,)), ((), ())), preferred_element_type=F32)


def dot_t(a, b):
    return lax.dot_general(a, b, (((1,), (1,)), ((), ())), preferred_element_type=F32)


def tick_kernel(
    n_section, n_dp, blocks, scale,
    up_index, down_index, tick_order, links,
    w_up, w_down, values_in, score_in, tangent_in, adjoint_in,
    saved_back, saved_tan, saved_second, saved_second_tan, saved_second_grad,
    v_out, g_out, grads_out,
    wu, wd, raw_x, raw_v, raw_c, x_slots, c_slots, xt, xs, cs,
    v0, v1, g1, v_sent, g_sent, v_last, g_last, grads,
    ys, yy, e0, e1, h0, h1, xy, rx, rc, ry, re, rxy, rcl, rel, crossing, crossed, total,
    chain, chain2, keep,
    in_sem, near_send, near_recv, send_sem, recv_sem, link_send, link_recv,
):
    section = lax.axis_index("section")
    me = lax.axis_index("dp")
    after = lax.rem(section + 1, n_section)
    before = lax.rem(section + n_section - 1, n_section)
    kept = blocks // n_dp
    row = n_dp // 2
    my_x, my_y = me % row, me // row
    across = (1 - my_y) * row + my_x

    loads = []

    def load(source, target):
        copy = pltpu.make_async_copy(source, target, in_sem.at[len(loads)])
        copy.start()
        loads.append(copy)

    for slot in range(2):
        for at, saved in enumerate((saved_back, saved_second, saved_second_tan, saved_tan)):
            load(saved.at[0, slot], raw_x.at[slot, pl.ds(8 * at, 8)])
    load(score_in.at[0], raw_c.at[pl.ds(0, 8)])
    load(adjoint_in.at[0], raw_c.at[pl.ds(8, 8)])
    for slot in range(2):
        load(saved_second_grad.at[0, slot], raw_c.at[pl.ds(16 + 8 * slot, 8)])
    early = len(loads)
    load(values_in.at[0], raw_v.at[pl.ds(0, 8)])
    load(tangent_in.at[0], raw_v.at[pl.ds(8, 8)])
    load(w_down.at[0], wd)
    load(w_up.at[0], wu)

    barrier = pltpu.get_barrier_semaphore()
    for p in range(1, n_dp):
        pl.semaphore_signal(barrier, inc=1, device_id={"dp": lax.rem(me + p, n_dp)}, device_id_type=MESH)
    for s in (after, before):
        pl.semaphore_signal(barrier, inc=1, device_id={"section": s}, device_id_type=MESH)

    first = tick_order[0, 0] * blocks
    later = tick_order[0, 1] * blocks

    chain[0] = jnp.zeros(chain.shape[1:], F32)
    chain2[0] = jnp.zeros(chain2.shape[1:], F32)

    for copy in loads[:early]:
        copy.wait()

    def to_blocks(j):
        here = cols(j)
        for slot in range(2):
            x_slots[slot * blocks + j] = raw_x[slot, :, here]
            c_slots[slot * blocks + j] = raw_c[pl.ds(16 + 8 * slot, 8), here]
        cs[j, pl.ds(0, 16)] = raw_c[pl.ds(0, 16), here]

    each_block(blocks, to_blocks)

    def gather_x(j):
        source = up_index[0, j]
        xs[j, pl.ds(0, 24)] = x_slots[first + source, pl.ds(0, 24)]
        xs[j, pl.ds(24, 8)] = x_slots[later + source, pl.ds(16, 8)]
        xy[j, pl.ds(0, 16)] = x_slots[later + source, pl.ds(0, 16)]
        cs[j, pl.ds(16, 8)] = c_slots[first + j]
        cs[j, pl.ds(24, 8)] = c_slots[later + j]

    each_block(blocks, gather_x)
    pl.semaphore_wait(barrier, n_dp + 1)

    sent = []

    near = []

    def slab(ref, d):
        return ref.at[pl.ds(d * kept, kept)]

    def spread_near(*parts):
        for side in (1, 0):
            for kind, source, landing in parts:
                for n, dx in enumerate(ALONG_X):
                    x = (my_x + dx) % row
                    peer = my_y * row + x
                    keeper = (my_y if side == 0 else 1 - my_y) * row + x
                    copy = pltpu.make_async_remote_copy(
                        src_ref=slab(source, keeper),
                        dst_ref=landing.at[side, my_x],
                        send_sem=near_send.at[kind, side, n],
                        recv_sem=near_recv.at[kind, side, n],
                        device_id={"dp": peer},
                        device_id_type=MESH,
                    )
                    copy.start()
                    near.append((side, copy))
        for kind, source, landing in parts:
            landing[0, my_x] = source[pl.ds(me * kept, kept)]
            landing[1, my_x] = source[pl.ds(across * kept, kept)]

    def spread(kind, source, landing):
        for n, (dx, dy) in enumerate(FAR_FIRST):
            peer = (my_y + dy) % 2 * row + (my_x + dx) % row
            copy = pltpu.make_async_remote_copy(
                src_ref=slab(source, peer),
                dst_ref=landing.at[me],
                send_sem=send_sem.at[kind, n],
                recv_sem=recv_sem.at[kind, n],
                device_id={"dp": peer},
                device_id_type=MESH,
            )
            copy.start()
            sent.append(copy)
        landing[me] = source[pl.ds(me * kept, kept)]

    spread_near((0, xs, rx), (1, cs, rc))

    for copy in loads[early : early + 2]:
        copy.wait()

    def to_blocks_v(j):
        v0[j] = raw_v[:, cols(j)]

    each_block(blocks, to_blocks_v)

    def gather_v(j):
        source = up_index[0, j]
        xt[j, pl.ds(0, 16)] = v0[source]
        xt[j, pl.ds(16, 8)] = x_slots[first + source, pl.ds(24, 8)]
        xt[j, pl.ds(24, 8)] = x_slots[later + source, pl.ds(24, 8)]

    each_block(blocks, gather_v)
    loads[early + 2].wait()

    def pull(i):
        chain[i + 1] = dot_t(cs[i], wd[i]) + chain[links[0, i]]

    each_block(blocks, pull)
    loads[early + 3].wait()

    def raise_all(j):
        z = dot(jnp.concatenate([xt[j], xs[j], xy[j, pl.ds(0, 16)]], 0), wu[j])
        zv, zt, tan_f, tan_l = z[0:8], z[8:16], z[16:24], z[24:32]
        back_f, za_f, ta_f = z[32:40], z[40:48], z[48:56]
        ta_l, back_l, za_l = z[56:64], z[64:72], z[72:80]
        pulled = chain[links[2, j]]
        pg, pa, ps_f, ps_l = pulled[0:8], pulled[8:16], pulled[16:24], pulled[24:32]
        sig_f, sig_l = logistic(za_f), logistic(za_l)
        slope_f, slope_l = slope_of(za_f, sig_f), slope_of(za_l, sig_l)
        sig_bf, sig_bl = logistic(back_f), logistic(back_l)
        hidden = silu_of(zv, logistic(zv))
        tangent_hidden = slope_of(tan_f, logistic(tan_f)) * zt
        h0[j] = jnp.concatenate([hidden, tangent_hidden], 0).astype(BF16)
        gate = slope_of(back_f, sig_bf) * pg
        push = slope_f * pa + curve_of(za_f, sig_f) * ps_f * ta_f
        e0[j] = jnp.concatenate([gate, push, slope_f * ps_f, slope_l * ps_l], 0).astype(BF16)
        yy[j] = jnp.concatenate(
            [
                silu_of(back_f, sig_bf),
                silu_of(za_f, sig_f),
                slope_f * ta_f,
                slope_l * ta_l,
                silu_of(back_l, sig_bl),
                silu_of(za_l, sig_l),
            ],
            0,
        ).astype(BF16)
        keep[j] = jnp.concatenate(
            [
                slope_of(back_l, sig_bl),
                slope_l,
                curve_of(za_l, sig_l) * ps_l * ta_l,
                slope_of(tan_l, logistic(tan_l)),
            ],
            0,
        )

    each_block(blocks, raise_all)

    def push_back(source):
        def body(j):
            chain2[j + 1] = dot_t(source[j, pl.ds(0, 16)], wu[j]) + chain2[links[1, j]]

        each_block(blocks, body)

    def settle(source, put):
        def body(b):
            put(b, (source[b, pl.ds(0, 16)].astype(F32) + chain2[links[3, b]]).astype(BF16))

        each_block(blocks, body)

    def lower(hidden, source, put):
        def body(i):
            put(i, (source[i].astype(F32) + dot(hidden[down_index[0, i]], wd[i])).astype(BF16))

        each_block(blocks, body)

    def in_block(ref):
        def put(i, value):
            ref[i] = value

        return put

    def in_rows(ref):
        def put(i, value):
            ref[0, :, cols(i)] = value[0:8]
            ref[1, :, cols(i)] = value[8:16]

        return put

    def relay(kind, source, landing, to):
        copy = pltpu.make_async_remote_copy(
            src_ref=source,
            dst_ref=landing,
            send_sem=link_send.at[kind],
            recv_sem=link_recv.at[kind],
            device_id={"section": to},
            device_id_type=MESH,
        )
        copy.start()
        return copy

    push_back(e0)
    settle(cs, in_block(g_sent))
    g_copy = relay(0, g_sent, g1, before)
    lower(h0, v0, in_block(v_sent))
    v_copy = relay(1, v_sent, v1, after)

    def gather_y(i):
        source = down_index[0, i]
        ys[i] = yy[source, pl.ds(0, 32)]
        xy[i, pl.ds(16, 16)] = yy[source, pl.ds(32, 16)]

    each_block(blocks, gather_y)
    spread_near((2, ys, ry), (3, e0, re))
    spread(0, xy, rxy)

    g_copy.wait_recv()
    spread(1, g1, rcl)

    def pull_later(i):
        chain[i + 1, pl.ds(0, 16)] = dot_t(g1[i], wd[i]) + chain[links[0, i], pl.ds(0, 16)]

    each_block(blocks, pull_later)

    def gate_later(j):
        pulled = chain[links[2, j], pl.ds(0, 16)]
        kept_rows = keep[j]
        gate = kept_rows[0:8] * pulled[0:8]
        push = kept_rows[8:16] * pulled[8:16] + kept_rows[16:24]
        e1[j] = jnp.concatenate([gate, push], 0).astype(BF16)

    each_block(blocks, gate_later)
    spread(2, e1, rel)

    push_back(e1)
    settle(g1, in_rows(g_last))
    g_end = relay(2, g_last, g_out, before)

    v_copy.wait_recv()

    def raise_later(j):
        z = dot(v1[up_index[0, j]], wu[j])
        zv, zt = z[0:8], z[8:16]
        h1[j] = jnp.concatenate([silu_of(zv, logistic(zv)), keep[j, pl.ds(24, 8)] * zt], 0).astype(BF16)

    each_block(blocks, raise_later)
    lower(h1, v1, in_rows(v_last))
    v_end = relay(3, v_last, v_out, after)

    def products(side, k):
        for half, (left, right) in enumerate(((rx, re), (ry, rc))):
            yield half, dot_rows(left[side, :, k].reshape(row * 32, BLOCK), right[side, :, k].reshape(row * 32, BLOCK))

    for side, copy in near:
        if side == 1:
            copy.wait_recv()
    for k in range(kept):
        for half, part in products(1, k):
            crossing[half, k] = part.astype(BF16)
    cross = pltpu.make_async_remote_copy(
        src_ref=crossing,
        dst_ref=crossed,
        send_sem=link_send.at[4],
        recv_sem=link_recv.at[4],
        device_id={"dp": across},
        device_id_type=MESH,
    )
    cross.start()
    for side, copy in near:
        if side == 0:
            copy.wait_recv()
    for k in range(kept):
        for half, part in products(0, k):
            total[half, k] = part
    for copy in sent:
        copy.wait_recv()
    cross.wait_recv()
    for k in range(kept):
        for half, right in enumerate((rel, rcl)):
            left = rxy[:, k, pl.ds(16 * half, 16)].reshape(n_dp * 16, BLOCK)
            part = dot_rows(left, right[:, k].reshape(n_dp * 16, BLOCK))
            grad = total[half, k] + crossed[half, k].astype(F32) + part
            grads[half, k] = (grad * scale).astype(BF16)

    grad_copy = pltpu.make_async_copy(grads, grads_out, in_sem.at[len(loads)])
    grad_copy.start()
    for copy in sent + [copy for _, copy in near] + [cross]:
        copy.wait_send()
    grad_copy.wait()
    g_copy.wait_send()
    v_copy.wait_send()
    g_end.wait()
    v_end.wait()


def hand_out(v, g, grads, values, score, tangent, adjoint, up, down, held, held_grads, in_sem, out_sem):
    moves = (
        (v, 0, values, held.at[0]),
        (v, 1, tangent, held.at[1]),
        (g, 0, score, held.at[2]),
        (g, 1, adjoint, held.at[3]),
        (grads, 0, up, held_grads.at[0]),
        (grads, 1, down, held_grads.at[1]),
    )
    inward = [
        pltpu.make_async_copy(source.at[half], stop, in_sem.at[n]) for n, (source, half, _, stop) in enumerate(moves)
    ]
    outward = [pltpu.make_async_copy(stop, target.at[0], out_sem.at[n]) for n, (_, _, target, stop) in enumerate(moves)]
    for copy in inward:
        copy.start()
    for arrived, copy in zip(inward, outward):
        arrived.wait()
        copy.start()
    for copy in outward:
        copy.wait()


def chain_links(down_index, up_index):
    index = jnp.concatenate([down_index, up_index], 0)
    count = index.shape[1]
    spot = jnp.arange(count, dtype=jnp.int32)
    own = jnp.concatenate([index, jnp.broadcast_to(spot, index.shape)], 0)
    over = jnp.concatenate([index, index], 0)
    limit = jnp.where(jnp.arange(4)[:, None] < 2, spot[None], count)
    hit = (own[:, :, None] == over[:, None, :]) & (spot[None, None, :] < limit[:, :, None])
    return jnp.max(jnp.where(hit, spot[None, None, :] + 1, 0), axis=2).astype(jnp.int32)


def on_device(mesh_shape, *arrays):
    (w_up, up_index, w_down, down_index, tick_order, *rest) = arrays
    n_section, n_dp = mesh_shape["section"], mesh_shape["dp"]
    blocks = w_up.shape[1]
    rows, width = rest[0].shape[1:]
    kept = blocks // n_dp
    links = chain_links(down_index, up_index)
    smem = pl.BlockSpec(memory_space=pltpu.SMEM)
    hbm = pl.BlockSpec(memory_space=pltpu.HBM)

    def by_block(height, copies=1):
        return pltpu.VMEM((copies * blocks, height, BLOCK), BF16)

    v, g, grads = pl.pallas_call(
        functools.partial(tick_kernel, n_section, n_dp, blocks, 1.0 / (rows * n_dp)),
        out_shape=(
            jax.ShapeDtypeStruct((2, rows, width), BF16),
            jax.ShapeDtypeStruct((2, rows, width), BF16),
            jax.ShapeDtypeStruct((2, kept, BLOCK, BLOCK), BF16),
        ),
        in_specs=[smem] * 4 + [hbm] * 11,
        out_specs=(hbm, hbm, hbm),
        scratch_shapes=[
            pltpu.VMEM((blocks, BLOCK, BLOCK), BF16),
            pltpu.VMEM((blocks, BLOCK, BLOCK), BF16),
            pltpu.VMEM((2, 32, width), BF16),
            pltpu.VMEM((16, width), BF16),
            pltpu.VMEM((32, width), BF16),
            by_block(32, 2),
            by_block(8, 2),
            by_block(32),
            by_block(32),
            by_block(32),
            *[by_block(16)] * 5,
            *[pltpu.VMEM((2, 8, width), BF16)] * 2,
            pltpu.VMEM((2, kept, BLOCK, BLOCK), BF16),
            by_block(32),
            by_block(48),
            by_block(32),
            *[by_block(16)] * 3,
            by_block(32),
            *[pltpu.VMEM((2, n_dp // 2, kept, 32, BLOCK), BF16)] * 4,
            pltpu.VMEM((n_dp, kept, 32, BLOCK), BF16),
            *[pltpu.VMEM((n_dp, kept, 16, BLOCK), BF16)] * 2,
            *[pltpu.VMEM((2, kept, BLOCK, BLOCK), BF16)] * 2,
            pltpu.VMEM((2, kept, BLOCK, BLOCK), F32),
            pltpu.VMEM((blocks + 1, 32, BLOCK), F32),
            pltpu.VMEM((blocks + 1, 16, BLOCK), F32),
            pltpu.VMEM((blocks, 32, BLOCK), F32),
            pltpu.SemaphoreType.DMA((17,)),
            *[pltpu.SemaphoreType.DMA((4, 2, len(ALONG_X)))] * 2,
            *[pltpu.SemaphoreType.DMA((3, n_dp - 1))] * 2,
            *[pltpu.SemaphoreType.DMA((5,))] * 2,
        ],
        compiler_params=pltpu.CompilerParams(
            collective_id=0, has_side_effects=True, vmem_limit_bytes=56 << 20
        ),
        name="ticks",
    )(up_index, down_index, tick_order, links, w_up, w_down, *rest)
    stream = jax.ShapeDtypeStruct((1, rows, width), BF16)
    grad = jax.ShapeDtypeStruct((1, kept, BLOCK, BLOCK), BF16)
    return pl.pallas_call(
        hand_out,
        out_shape=(stream,) * 4 + (grad,) * 2,
        in_specs=[hbm] * 3,
        out_specs=(hbm,) * 6,
        scratch_shapes=[
            pltpu.VMEM((4, rows, width), BF16),
            pltpu.VMEM((2, kept, BLOCK, BLOCK), BF16),
            pltpu.SemaphoreType.DMA((6,)),
            pltpu.SemaphoreType.DMA((6,)),
        ],
        compiler_params=pltpu.CompilerParams(vmem_limit_bytes=56 << 20),
        name="hand_out",
    )(v, g, grads)


def solution(mesh):
    matrix = P("section", None, None, None)
    table = P("section", None)
    stream = P("section", "dp", None)
    saved = P("section", None, "dp", None)
    return jax.shard_map(
        functools.partial(on_device, dict(mesh.shape)),
        mesh=mesh,
        in_specs=(matrix, table, matrix, table, table) + (stream,) * 4 + (saved,) * 5,
        out_specs=(stream,) * 4 + (P("section", "dp", None, None),) * 2,
        check_vma=False,
    )
```

```python
import functools

import jax
import jax.numpy as jnp
from jax import lax
from jax.experimental import pallas as pl
from jax.experimental.pallas import tpu as pltpu
from jax.sharding import PartitionSpec as P

BLOCK = 128
UNROLL = 32
ALONG_X = (2, 1, 3)
FAR_FIRST = ((2, 1), (2, 0), (1, 1), (1, 0), (3, 1), (3, 0), (0, 1))
MESH = pl.DeviceIdType.MESH
F32 = jnp.float32
BF16 = jnp.bfloat16


def logistic(z):
    return 0.5 * jnp.tanh(0.5 * z) + 0.5


def silu_of(z, sig):
    return z * sig


def slope_of(z, sig):
    return sig * (1.0 + z * (1.0 - sig))


def curve_of(z, sig):
    return sig * (1.0 - sig) * (2.0 + z * (1.0 - 2.0 * sig))


def cols(i, width=BLOCK):
    return pl.ds(pl.multiple_of(i * width, width), width)


def each_block(count, body):
    def step(i, carry):
        body(i)
        return carry

    lax.fori_loop(0, count, step, 0, unroll=UNROLL)


def dot(a, b):
    return jnp.dot(a, b, preferred_element_type=F32)


def dot_rows(a, b):
    return lax.dot_general(a, b, (((0,), (0,)), ((), ())), preferred_element_type=F32)


def dot_t(a, b):
    return lax.dot_general(a, b, (((1,), (1,)), ((), ())), preferred_element_type=F32)


def tick_kernel(
    n_section, n_dp, blocks, scale,
    up_index, down_index, tick_order, up_row, down_row,
    w_up, w_down, values_in, score_in, tangent_in, adjoint_in,
    saved_back, saved_tan, saved_second, saved_second_tan, saved_second_grad,
    v_out, g_out, grads_out,
    wu, wd, raw_x, raw_v, raw_c, x_slots, c_slots, xt, xs, cs,
    v0, v1, g1, v_sent, g_sent, v_last, g_last, grads,
    ys, yy, e0, e1, h0, h1, xy, rx, rc, ry, re, rxy, rcl, rel, crossing, crossed, total,
    chain, chain2, keep, links_row, links,
    in_sem, near_send, near_recv, send_sem, recv_sem, link_send, link_recv,
):
    section = lax.axis_index("section")
    me = lax.axis_index("dp")
    after = lax.rem(section + 1, n_section)
    before = lax.rem(section + n_section - 1, n_section)
    kept = blocks // n_dp
    row = n_dp // 2
    my_x, my_y = me % row, me // row
    across = (1 - my_y) * row + my_x

    loads = []

    def load(source, target):
        copy = pltpu.make_async_copy(source, target, in_sem.at[len(loads)])
        copy.start()
        loads.append(copy)

    for slot in range(2):
        for at, saved in enumerate((saved_back, saved_second, saved_second_tan, saved_tan)):
            load(saved.at[0, slot], raw_x.at[slot, pl.ds(8 * at, 8)])
    load(score_in.at[0], raw_c.at[pl.ds(0, 8)])
    load(adjoint_in.at[0], raw_c.at[pl.ds(8, 8)])
    for slot in range(2):
        load(saved_second_grad.at[0, slot], raw_c.at[pl.ds(16 + 8 * slot, 8)])
    early = len(loads)
    load(values_in.at[0], raw_v.at[pl.ds(0, 8)])
    load(tangent_in.at[0], raw_v.at[pl.ds(8, 8)])
    load(w_down.at[0], wd)
    load(w_up.at[0], wu)

    barrier = pltpu.get_barrier_semaphore()
    for p in range(1, n_dp):
        pl.semaphore_signal(barrier, inc=1, device_id={"dp": lax.rem(me + p, n_dp)}, device_id_type=MESH)
    for s in (after, before):
        pl.semaphore_signal(barrier, inc=1, device_id={"section": s}, device_id_type=MESH)

    rows = lax.broadcasted_iota(jnp.int32, (blocks, blocks), 0)
    lanes = lax.broadcasted_iota(jnp.int32, (blocks, blocks), 1)
    for at, index in enumerate((down_row, up_row)):
        over = jnp.broadcast_to(index[...], (blocks, blocks))
        down = jnp.max(jnp.where(rows == lanes, over, 0), axis=1, keepdims=True)
        same = (down == over) & (rows < lanes)
        links_row[pl.ds(at, 1)] = jnp.max(jnp.where(same, rows + 1, 0), axis=0, keepdims=True)
        links_row[pl.ds(2 + at, 1)] = jnp.max(jnp.where(down == lanes, rows + 1, 0), axis=0, keepdims=True)
    links_copy = pltpu.make_async_copy(links_row, links, in_sem.at[len(loads) + 1])
    links_copy.start()

    first = tick_order[0, 0] * blocks
    later = tick_order[0, 1] * blocks

    chain[0] = jnp.zeros(chain.shape[1:], F32)
    chain2[0] = jnp.zeros(chain2.shape[1:], F32)

    for copy in loads[:early]:
        copy.wait()

    def to_blocks(j):
        here = cols(j)
        for slot in range(2):
            x_slots[slot * blocks + j] = raw_x[slot, :, here]
            c_slots[slot * blocks + j] = raw_c[pl.ds(16 + 8 * slot, 8), here]
        cs[j, pl.ds(0, 16)] = raw_c[pl.ds(0, 16), here]

    each_block(blocks, to_blocks)

    def gather_x(j):
        source = up_index[0, j]
        xs[j, pl.ds(0, 24)] = x_slots[first + source, pl.ds(0, 24)]
        xs[j, pl.ds(24, 8)] = x_slots[later + source, pl.ds(16, 8)]
        xy[j, pl.ds(0, 16)] = x_slots[later + source, pl.ds(0, 16)]
        cs[j, pl.ds(16, 8)] = c_slots[first + j]
        cs[j, pl.ds(24, 8)] = c_slots[later + j]

    each_block(blocks, gather_x)
    pl.semaphore_wait(barrier, n_dp + 1)

    sent = []

    near = []

    def slab(ref, d):
        return ref.at[pl.ds(d * kept, kept)]

    def spread_near(*parts):
        for side in (1, 0):
            for kind, source, landing in parts:
                for n, dx in enumerate(ALONG_X):
                    x = (my_x + dx) % row
                    peer = my_y * row + x
                    keeper = (my_y if side == 0 else 1 - my_y) * row + x
                    copy = pltpu.make_async_remote_copy(
                        src_ref=slab(source, keeper),
                        dst_ref=landing.at[side, my_x],
                        send_sem=near_send.at[kind, side, n],
                        recv_sem=near_recv.at[kind, side, n],
                        device_id={"dp": peer},
                        device_id_type=MESH,
                    )
                    copy.start()
                    near.append((side, copy))
        for kind, source, landing in parts:
            landing[0, my_x] = source[pl.ds(me * kept, kept)]
            landing[1, my_x] = source[pl.ds(across * kept, kept)]

    def spread(kind, source, landing):
        for n, (dx, dy) in enumerate(FAR_FIRST):
            peer = (my_y + dy) % 2 * row + (my_x + dx) % row
            copy = pltpu.make_async_remote_copy(
                src_ref=slab(source, peer),
                dst_ref=landing.at[me],
                send_sem=send_sem.at[kind, n],
                recv_sem=recv_sem.at[kind, n],
                device_id={"dp": peer},
                device_id_type=MESH,
            )
            copy.start()
            sent.append(copy)
        landing[me] = source[pl.ds(me * kept, kept)]

    spread_near((0, xs, rx), (1, cs, rc))

    for copy in loads[early : early + 2]:
        copy.wait()

    def to_blocks_v(j):
        v0[j] = raw_v[:, cols(j)]

    each_block(blocks, to_blocks_v)

    def gather_v(j):
        source = up_index[0, j]
        xt[j, pl.ds(0, 16)] = v0[source]
        xt[j, pl.ds(16, 8)] = x_slots[first + source, pl.ds(24, 8)]
        xt[j, pl.ds(24, 8)] = x_slots[later + source, pl.ds(24, 8)]

    each_block(blocks, gather_v)
    links_copy.wait()
    loads[early + 2].wait()

    def pull(i):
        chain[i + 1] = dot_t(cs[i], wd[i]) + chain[links[0, i]]

    each_block(blocks, pull)
    loads[early + 3].wait()

    def raise_first(j):
        z = dot(jnp.concatenate([xt[j, pl.ds(0, 24)], xs[j, pl.ds(0, 24)]], 0), wu[j])
        zv, zt, tan, back, za, ta = (z[8 * n : 8 * n + 8] for n in range(6))
        pulled = chain[links[2, j]]
        pg, pa, ps = pulled[0:8], pulled[8:16], pulled[16:24]
        sig, sig_back = logistic(za), logistic(back)
        slope = slope_of(za, sig)
        hidden = silu_of(zv, logistic(zv))
        tangent_hidden = slope_of(tan, logistic(tan)) * zt
        h0[j] = jnp.concatenate([hidden, tangent_hidden], 0).astype(BF16)
        gate = slope_of(back, sig_back) * pg
        push = slope * pa + curve_of(za, sig) * ps * ta
        e0[j, pl.ds(0, 16)] = jnp.concatenate([gate, push], 0).astype(BF16)
        e0[j, pl.ds(16, 8)] = (slope * ps).astype(BF16)
        yy[j, pl.ds(0, 16)] = jnp.concatenate([silu_of(back, sig_back), silu_of(za, sig)], 0).astype(BF16)
        yy[j, pl.ds(16, 8)] = (slope * ta).astype(BF16)

    each_block(blocks, raise_first)

    def raise_saved(j):
        rows = jnp.concatenate([xt[j, pl.ds(24, 8)], xs[j, pl.ds(24, 8)], xy[j, pl.ds(0, 16)]], 0)
        z = dot(rows, wu[j])
        tan, ta, back, za = (z[8 * n : 8 * n + 8] for n in range(4))
        ps = chain[links[2, j], pl.ds(24, 8)]
        sig, sig_back = logistic(za), logistic(back)
        slope = slope_of(za, sig)
        e0[j, pl.ds(24, 8)] = (slope * ps).astype(BF16)
        yy[j, pl.ds(24, 8)] = (slope * ta).astype(BF16)
        yy[j, pl.ds(32, 16)] = jnp.concatenate([silu_of(back, sig_back), silu_of(za, sig)], 0).astype(BF16)
        keep[j] = jnp.concatenate(
            [slope_of(back, sig_back), slope, curve_of(za, sig) * ps * ta, slope_of(tan, logistic(tan))], 0
        )

    def push_back(source):
        def body(j):
            chain2[j + 1] = dot_t(source[j, pl.ds(0, 16)], wu[j]) + chain2[links[1, j]]

        each_block(blocks, body)

    def settle(source, put):
        def body(b):
            put(b, (source[b, pl.ds(0, 16)].astype(F32) + chain2[links[3, b]]).astype(BF16))

        each_block(blocks, body)

    def lower(hidden, source, put):
        def body(i):
            put(i, (source[i].astype(F32) + dot(hidden[down_index[0, i]], wd[i])).astype(BF16))

        each_block(blocks, body)

    def in_block(ref):
        def put(i, value):
            ref[i] = value

        return put

    def in_rows(ref):
        def put(i, value):
            ref[0, :, cols(i)] = value[0:8]
            ref[1, :, cols(i)] = value[8:16]

        return put

    def relay(kind, source, landing, to):
        copy = pltpu.make_async_remote_copy(
            src_ref=source,
            dst_ref=landing,
            send_sem=link_send.at[kind],
            recv_sem=link_recv.at[kind],
            device_id={"section": to},
            device_id_type=MESH,
        )
        copy.start()
        return copy

    push_back(e0)
    settle(cs, in_block(g_sent))
    g_copy = relay(0, g_sent, g1, before)
    lower(h0, v0, in_block(v_sent))
    v_copy = relay(1, v_sent, v1, after)

    each_block(blocks, raise_saved)

    def gather_y(i):
        source = down_index[0, i]
        ys[i] = yy[source, pl.ds(0, 32)]
        xy[i, pl.ds(16, 16)] = yy[source, pl.ds(32, 16)]

    each_block(blocks, gather_y)
    spread_near((2, ys, ry), (3, e0, re))
    spread(0, xy, rxy)

    g_copy.wait_recv()
    spread(1, g1, rcl)

    def pull_later(i):
        chain[i + 1, pl.ds(0, 16)] = dot_t(g1[i], wd[i]) + chain[links[0, i], pl.ds(0, 16)]

    each_block(blocks, pull_later)

    def gate_later(j):
        pulled = chain[links[2, j], pl.ds(0, 16)]
        kept_rows = keep[j]
        gate = kept_rows[0:8] * pulled[0:8]
        push = kept_rows[8:16] * pulled[8:16] + kept_rows[16:24]
        e1[j] = jnp.concatenate([gate, push], 0).astype(BF16)

    each_block(blocks, gate_later)
    spread(2, e1, rel)

    push_back(e1)
    settle(g1, in_rows(g_last))
    g_end = relay(2, g_last, g_out, before)

    v_copy.wait_recv()

    def raise_later(j):
        z = dot(v1[up_index[0, j]], wu[j])
        zv, zt = z[0:8], z[8:16]
        h1[j] = jnp.concatenate([silu_of(zv, logistic(zv)), keep[j, pl.ds(24, 8)] * zt], 0).astype(BF16)

    each_block(blocks, raise_later)
    lower(h1, v1, in_rows(v_last))
    v_end = relay(3, v_last, v_out, after)

    def products(side, k):
        for half, (left, right) in enumerate(((rx, re), (ry, rc))):
            yield half, dot_rows(left[side, :, k].reshape(row * 32, BLOCK), right[side, :, k].reshape(row * 32, BLOCK))

    for side, copy in near:
        if side == 1:
            copy.wait_recv()
    for k in range(kept):
        for half, part in products(1, k):
            crossing[half, k] = part.astype(BF16)
    cross = pltpu.make_async_remote_copy(
        src_ref=crossing,
        dst_ref=crossed,
        send_sem=link_send.at[4],
        recv_sem=link_recv.at[4],
        device_id={"dp": across},
        device_id_type=MESH,
    )
    cross.start()
    for side, copy in near:
        if side == 0:
            copy.wait_recv()
    for k in range(kept):
        for half, part in products(0, k):
            total[half, k] = part
    for copy in sent:
        copy.wait_recv()
    cross.wait_recv()
    for k in range(kept):
        for half, right in enumerate((rel, rcl)):
            left = rxy[:, k, pl.ds(16 * half, 16)].reshape(n_dp * 16, BLOCK)
            part = dot_rows(left, right[:, k].reshape(n_dp * 16, BLOCK))
            grad = total[half, k] + crossed[half, k].astype(F32) + part
            grads[half, k] = (grad * scale).astype(BF16)

    grad_copy = pltpu.make_async_copy(grads, grads_out, in_sem.at[len(loads)])
    grad_copy.start()
    for copy in sent + [copy for _, copy in near] + [cross]:
        copy.wait_send()
    grad_copy.wait()
    g_copy.wait_send()
    v_copy.wait_send()
    g_end.wait()
    v_end.wait()


def hand_out(v, g, grads, values, score, tangent, adjoint, up, down, held, held_grads, in_sem, out_sem):
    moves = (
        (v, 0, values, held.at[0]),
        (v, 1, tangent, held.at[1]),
        (g, 0, score, held.at[2]),
        (g, 1, adjoint, held.at[3]),
        (grads, 0, up, held_grads.at[0]),
        (grads, 1, down, held_grads.at[1]),
    )
    inward = [
        pltpu.make_async_copy(source.at[half], stop, in_sem.at[n]) for n, (source, half, _, stop) in enumerate(moves)
    ]
    outward = [pltpu.make_async_copy(stop, target.at[0], out_sem.at[n]) for n, (_, _, target, stop) in enumerate(moves)]
    for copy in inward:
        copy.start()
    for arrived, copy in zip(inward, outward):
        arrived.wait()
        copy.start()
    for copy in outward:
        copy.wait()


def on_device(mesh_shape, *arrays):
    (w_up, up_index, w_down, down_index, tick_order, *rest) = arrays
    n_section, n_dp = mesh_shape["section"], mesh_shape["dp"]
    blocks = w_up.shape[1]
    rows, width = rest[0].shape[1:]
    kept = blocks // n_dp
    smem = pl.BlockSpec(memory_space=pltpu.SMEM)
    hbm = pl.BlockSpec(memory_space=pltpu.HBM)
    vmem = pl.BlockSpec(memory_space=pltpu.VMEM)

    def by_block(height, copies=1):
        return pltpu.VMEM((copies * blocks, height, BLOCK), BF16)

    v, g, grads = pl.pallas_call(
        functools.partial(tick_kernel, n_section, n_dp, blocks, 1.0 / (rows * n_dp)),
        out_shape=(
            jax.ShapeDtypeStruct((2, rows, width), BF16),
            jax.ShapeDtypeStruct((2, rows, width), BF16),
            jax.ShapeDtypeStruct((2, kept, BLOCK, BLOCK), BF16),
        ),
        in_specs=[smem] * 3 + [vmem] * 2 + [hbm] * 11,
        out_specs=(hbm, hbm, hbm),
        scratch_shapes=[
            pltpu.VMEM((blocks, BLOCK, BLOCK), BF16),
            pltpu.VMEM((blocks, BLOCK, BLOCK), BF16),
            pltpu.VMEM((2, 32, width), BF16),
            pltpu.VMEM((16, width), BF16),
            pltpu.VMEM((32, width), BF16),
            by_block(32, 2),
            by_block(8, 2),
            by_block(32),
            by_block(32),
            by_block(32),
            *[by_block(16)] * 5,
            *[pltpu.VMEM((2, 8, width), BF16)] * 2,
            pltpu.VMEM((2, kept, BLOCK, BLOCK), BF16),
            by_block(32),
            by_block(48),
            by_block(32),
            *[by_block(16)] * 3,
            by_block(32),
            *[pltpu.VMEM((2, n_dp // 2, kept, 32, BLOCK), BF16)] * 4,
            pltpu.VMEM((n_dp, kept, 32, BLOCK), BF16),
            *[pltpu.VMEM((n_dp, kept, 16, BLOCK), BF16)] * 2,
            *[pltpu.VMEM((2, kept, BLOCK, BLOCK), BF16)] * 2,
            pltpu.VMEM((2, kept, BLOCK, BLOCK), F32),
            pltpu.VMEM((blocks + 1, 32, BLOCK), F32),
            pltpu.VMEM((blocks + 1, 16, BLOCK), F32),
            pltpu.VMEM((blocks, 32, BLOCK), F32),
            pltpu.VMEM((4, blocks), jnp.int32),
            pltpu.SMEM((4, blocks), jnp.int32),
            pltpu.SemaphoreType.DMA((18,)),
            *[pltpu.SemaphoreType.DMA((4, 2, len(ALONG_X)))] * 2,
            *[pltpu.SemaphoreType.DMA((3, n_dp - 1))] * 2,
            *[pltpu.SemaphoreType.DMA((5,))] * 2,
        ],
        compiler_params=pltpu.CompilerParams(
            collective_id=0, has_side_effects=True, vmem_limit_bytes=56 << 20
        ),
        name="ticks",
    )(up_index, down_index, tick_order, up_index, down_index, w_up, w_down, *rest)
    stream = jax.ShapeDtypeStruct((1, rows, width), BF16)
    grad = jax.ShapeDtypeStruct((1, kept, BLOCK, BLOCK), BF16)
    return pl.pallas_call(
        hand_out,
        out_shape=(stream,) * 4 + (grad,) * 2,
        in_specs=[hbm] * 3,
        out_specs=(hbm,) * 6,
        scratch_shapes=[
            pltpu.VMEM((4, rows, width), BF16),
            pltpu.VMEM((2, kept, BLOCK, BLOCK), BF16),
            pltpu.SemaphoreType.DMA((6,)),
            pltpu.SemaphoreType.DMA((6,)),
        ],
        compiler_params=pltpu.CompilerParams(vmem_limit_bytes=56 << 20),
        name="hand_out",
    )(v, g, grads)


def solution(mesh):
    matrix = P("section", None, None, None)
    table = P("section", None)
    stream = P("section", "dp", None)
    saved = P("section", None, "dp", None)
    return jax.shard_map(
        functools.partial(on_device, dict(mesh.shape)),
        mesh=mesh,
        in_specs=(matrix, table, matrix, table, table) + (stream,) * 4 + (saved,) * 5,
        out_specs=(stream,) * 4 + (P("section", "dp", None, None),) * 2,
        check_vma=False,
    )
```

```python
import functools

import jax
import jax.numpy as jnp
from jax import lax
from jax.experimental import pallas as pl
from jax.experimental.pallas import tpu as pltpu
from jax.sharding import PartitionSpec as P

BLOCK = 128
UNROLL = 32
ALONG_X = (2, 1, 3)
FAR_FIRST = ((2, 1), (2, 0), (1, 1), (1, 0), (3, 1), (3, 0), (0, 1))
MESH = pl.DeviceIdType.MESH
F32 = jnp.float32
BF16 = jnp.bfloat16


def logistic(z):
    return 0.5 * jnp.tanh(0.5 * z) + 0.5


def silu_of(z, sig):
    return z * sig


def slope_of(z, sig):
    return sig * (1.0 + z * (1.0 - sig))


def curve_of(z, sig):
    return sig * (1.0 - sig) * (2.0 + z * (1.0 - 2.0 * sig))


def cols(i, width=BLOCK):
    return pl.ds(pl.multiple_of(i * width, width), width)


def each_block(count, body):
    def step(i, carry):
        body(i)
        return carry

    lax.fori_loop(0, count, step, 0, unroll=UNROLL)


def dot(a, b):
    return jnp.dot(a, b, preferred_element_type=F32)


def dot_rows(a, b):
    return lax.dot_general(a, b, (((0,), (0,)), ((), ())), preferred_element_type=F32)


def dot_t(a, b):
    return lax.dot_general(a, b, (((1,), (1,)), ((), ())), preferred_element_type=F32)


def tick_kernel(
    n_section, n_dp, blocks, scale,
    up_index, down_index, tick_order, up_row, down_row,
    w_up, w_down, values_in, score_in, tangent_in, adjoint_in,
    saved_back, saved_tan, saved_second, saved_second_tan, saved_second_grad,
    v_out, g_out, grads_out,
    wu, wd, raw_x, raw_v, raw_c, x_slots, c_slots, xt, xs, cs,
    v0, v1, g1, v_sent, g_sent, v_last, g_last,
    ys, yy, e0, e1, h0, h1, xy, rx, rc, ry, re, rxy, rcl, rel, crossing, crossed, total,
    chain, chain2, keep, links_row, links,
    in_sem, near_send, near_recv, send_sem, recv_sem, link_send, link_recv,
):
    section = lax.axis_index("section")
    me = lax.axis_index("dp")
    after = lax.rem(section + 1, n_section)
    before = lax.rem(section + n_section - 1, n_section)
    kept = blocks // n_dp
    row = n_dp // 2
    my_x, my_y = me % row, me // row
    across = (1 - my_y) * row + my_x

    barrier = pltpu.get_barrier_semaphore()
    for p in range(1, n_dp):
        pl.semaphore_signal(barrier, inc=1, device_id={"dp": lax.rem(me + p, n_dp)}, device_id_type=MESH)
    for s in (after, before):
        pl.semaphore_signal(barrier, inc=1, device_id={"section": s}, device_id_type=MESH)

    loads = []

    def load(source, target):
        copy = pltpu.make_async_copy(source, target, in_sem.at[len(loads)])
        copy.start()
        loads.append(copy)

    for slot in range(2):
        for at, saved in enumerate((saved_back, saved_second, saved_second_tan, saved_tan)):
            load(saved.at[0, slot], raw_x.at[slot, pl.ds(8 * at, 8)])
    load(score_in.at[0], raw_c.at[pl.ds(0, 8)])
    load(adjoint_in.at[0], raw_c.at[pl.ds(8, 8)])
    for slot in range(2):
        load(saved_second_grad.at[0, slot], raw_c.at[pl.ds(16 + 8 * slot, 8)])
    early = len(loads)
    load(values_in.at[0], raw_v.at[pl.ds(0, 8)])
    load(tangent_in.at[0], raw_v.at[pl.ds(8, 8)])
    load(w_down.at[0], wd)
    load(w_up.at[0], wu)

    rows = lax.broadcasted_iota(jnp.int32, (blocks, blocks), 0)
    lanes = lax.broadcasted_iota(jnp.int32, (blocks, blocks), 1)
    for at, index in enumerate((down_row, up_row)):
        over = jnp.broadcast_to(index[...], (blocks, blocks))
        down = jnp.max(jnp.where(rows == lanes, over, 0), axis=1, keepdims=True)
        same = (down == over) & (rows < lanes)
        links_row[pl.ds(at, 1)] = jnp.max(jnp.where(same, rows + 1, 0), axis=0, keepdims=True)
        links_row[pl.ds(2 + at, 1)] = jnp.max(jnp.where(down == lanes, rows + 1, 0), axis=0, keepdims=True)
    links_copy = pltpu.make_async_copy(links_row, links, in_sem.at[len(loads)])
    links_copy.start()

    first = tick_order[0, 0] * blocks
    later = tick_order[0, 1] * blocks

    chain[0] = jnp.zeros(chain.shape[1:], F32)
    chain2[0] = jnp.zeros(chain2.shape[1:], F32)

    for copy in loads[:early]:
        copy.wait()

    def to_blocks(j):
        here = cols(j)
        for slot in range(2):
            x_slots[slot * blocks + j] = raw_x[slot, :, here]
            c_slots[slot * blocks + j] = raw_c[pl.ds(16 + 8 * slot, 8), here]
        cs[j, pl.ds(0, 16)] = raw_c[pl.ds(0, 16), here]

    each_block(blocks, to_blocks)

    def gather_x(j):
        source = up_index[0, j]
        xs[j, pl.ds(0, 24)] = x_slots[first + source, pl.ds(0, 24)]
        xs[j, pl.ds(24, 8)] = x_slots[later + source, pl.ds(16, 8)]
        xy[j, pl.ds(0, 16)] = x_slots[later + source, pl.ds(0, 16)]
        cs[j, pl.ds(16, 8)] = c_slots[first + j]
        cs[j, pl.ds(24, 8)] = c_slots[later + j]

    each_block(blocks, gather_x)
    pl.semaphore_wait(barrier, n_dp + 1)

    sent = []

    near = []

    def slab(ref, d):
        return ref.at[pl.ds(d * kept, kept)]

    def spread_near(*parts):
        for side in (1, 0):
            for kind, source, landing in parts:
                for n, dx in enumerate(ALONG_X):
                    x = (my_x + dx) % row
                    peer = my_y * row + x
                    keeper = (my_y if side == 0 else 1 - my_y) * row + x
                    copy = pltpu.make_async_remote_copy(
                        src_ref=slab(source, keeper),
                        dst_ref=landing.at[side, my_x],
                        send_sem=near_send.at[kind, side, n],
                        recv_sem=near_recv.at[kind, side, n],
                        device_id={"dp": peer},
                        device_id_type=MESH,
                    )
                    copy.start()
                    near.append((side, copy))
        for kind, source, landing in parts:
            landing[0, my_x] = source[pl.ds(me * kept, kept)]
            landing[1, my_x] = source[pl.ds(across * kept, kept)]

    def spread(kind, source, landing):
        for n, (dx, dy) in enumerate(FAR_FIRST):
            peer = (my_y + dy) % 2 * row + (my_x + dx) % row
            copy = pltpu.make_async_remote_copy(
                src_ref=slab(source, peer),
                dst_ref=landing.at[me],
                send_sem=send_sem.at[kind, n],
                recv_sem=recv_sem.at[kind, n],
                device_id={"dp": peer},
                device_id_type=MESH,
            )
            copy.start()
            sent.append(copy)
        landing[me] = source[pl.ds(me * kept, kept)]

    spread_near((0, xs, rx), (1, cs, rc))

    for copy in loads[early : early + 2]:
        copy.wait()

    def to_blocks_v(j):
        v0[j] = raw_v[:, cols(j)]

    each_block(blocks, to_blocks_v)

    def gather_v(j):
        source = up_index[0, j]
        xt[j, pl.ds(0, 16)] = v0[source]
        xt[j, pl.ds(16, 8)] = x_slots[first + source, pl.ds(24, 8)]
        xt[j, pl.ds(24, 8)] = x_slots[later + source, pl.ds(24, 8)]

    each_block(blocks, gather_v)
    links_copy.wait()
    loads[early + 2].wait()

    def pull(i):
        chain[i + 1] = dot_t(cs[i], wd[i]) + chain[links[0, i]]

    each_block(blocks, pull)
    loads[early + 3].wait()

    def raise_first(j):
        z = dot(jnp.concatenate([xt[j, pl.ds(0, 24)], xs[j, pl.ds(0, 24)]], 0), wu[j])
        zv, zt, tan, back, za, ta = (z[8 * n : 8 * n + 8] for n in range(6))
        pulled = chain[links[2, j]]
        pg, pa, ps = pulled[0:8], pulled[8:16], pulled[16:24]
        sig, sig_back = logistic(za), logistic(back)
        slope = slope_of(za, sig)
        hidden = silu_of(zv, logistic(zv))
        tangent_hidden = slope_of(tan, logistic(tan)) * zt
        h0[j] = jnp.concatenate([hidden, tangent_hidden], 0).astype(BF16)
        gate = slope_of(back, sig_back) * pg
        push = slope * pa + curve_of(za, sig) * ps * ta
        e0[j, pl.ds(0, 16)] = jnp.concatenate([gate, push], 0).astype(BF16)
        e0[j, pl.ds(16, 8)] = (slope * ps).astype(BF16)
        yy[j, pl.ds(0, 16)] = jnp.concatenate([silu_of(back, sig_back), silu_of(za, sig)], 0).astype(BF16)
        yy[j, pl.ds(16, 8)] = (slope * ta).astype(BF16)

    each_block(blocks, raise_first)

    def raise_saved(j):
        rows = jnp.concatenate([xt[j, pl.ds(24, 8)], xs[j, pl.ds(24, 8)], xy[j, pl.ds(0, 16)]], 0)
        z = dot(rows, wu[j])
        tan, ta, back, za = (z[8 * n : 8 * n + 8] for n in range(4))
        ps = chain[links[2, j], pl.ds(24, 8)]
        sig, sig_back = logistic(za), logistic(back)
        slope = slope_of(za, sig)
        e0[j, pl.ds(24, 8)] = (slope * ps).astype(BF16)
        yy[j, pl.ds(24, 8)] = (slope * ta).astype(BF16)
        yy[j, pl.ds(32, 16)] = jnp.concatenate([silu_of(back, sig_back), silu_of(za, sig)], 0).astype(BF16)
        keep[j] = jnp.concatenate(
            [slope_of(back, sig_back), slope, curve_of(za, sig) * ps * ta, slope_of(tan, logistic(tan))], 0
        )

    def push_back(source):
        def body(j):
            chain2[j + 1] = dot_t(source[j, pl.ds(0, 16)], wu[j]) + chain2[links[1, j]]

        each_block(blocks, body)

    def settle(source, put):
        def body(b):
            put(b, (source[b, pl.ds(0, 16)].astype(F32) + chain2[links[3, b]]).astype(BF16))

        each_block(blocks, body)

    def lower(hidden, source, put):
        def body(i):
            put(i, (source[i].astype(F32) + dot(hidden[down_index[0, i]], wd[i])).astype(BF16))

        each_block(blocks, body)

    def in_block(ref):
        def put(i, value):
            ref[i] = value

        return put

    def in_rows(ref):
        def put(i, value):
            ref[0, :, cols(i)] = value[0:8]
            ref[1, :, cols(i)] = value[8:16]

        return put

    def relay(kind, source, landing, to):
        copy = pltpu.make_async_remote_copy(
            src_ref=source,
            dst_ref=landing,
            send_sem=link_send.at[kind],
            recv_sem=link_recv.at[kind],
            device_id={"section": to},
            device_id_type=MESH,
        )
        copy.start()
        return copy

    push_back(e0)
    settle(cs, in_block(g_sent))
    g_copy = relay(0, g_sent, g1, before)
    lower(h0, v0, in_block(v_sent))
    v_copy = relay(1, v_sent, v1, after)

    each_block(blocks, raise_saved)

    def gather_y(i):
        source = down_index[0, i]
        ys[i] = yy[source, pl.ds(0, 32)]
        xy[i, pl.ds(16, 16)] = yy[source, pl.ds(32, 16)]

    each_block(blocks, gather_y)
    spread_near((2, ys, ry), (3, e0, re))
    spread(0, xy, rxy)

    g_copy.wait_recv()
    spread(1, g1, rcl)

    def pull_later(i):
        chain[i + 1, pl.ds(0, 16)] = dot_t(g1[i], wd[i]) + chain[links[0, i], pl.ds(0, 16)]

    each_block(blocks, pull_later)

    def gate_later(j):
        pulled = chain[links[2, j], pl.ds(0, 16)]
        kept_rows = keep[j]
        gate = kept_rows[0:8] * pulled[0:8]
        push = kept_rows[8:16] * pulled[8:16] + kept_rows[16:24]
        e1[j] = jnp.concatenate([gate, push], 0).astype(BF16)

    each_block(blocks, gate_later)
    spread(2, e1, rel)

    push_back(e1)
    settle(g1, in_rows(g_last))
    g_end = relay(2, g_last, g_out, before)

    v_copy.wait_recv()

    def raise_later(j):
        z = dot(v1[up_index[0, j]], wu[j])
        zv, zt = z[0:8], z[8:16]
        h1[j] = jnp.concatenate([silu_of(zv, logistic(zv)), keep[j, pl.ds(24, 8)] * zt], 0).astype(BF16)

    each_block(blocks, raise_later)
    lower(h1, v1, in_rows(v_last))
    v_end = relay(3, v_last, v_out, after)

    def products(side, k):
        for half, (left, right) in enumerate(((rx, re), (ry, rc))):
            yield half, dot_rows(left[side, :, k].reshape(row * 32, BLOCK), right[side, :, k].reshape(row * 32, BLOCK))

    for side, copy in near:
        if side == 1:
            copy.wait_recv()
    for k in range(kept):
        for half, part in products(1, k):
            crossing[half, k] = part.astype(BF16)
    cross = pltpu.make_async_remote_copy(
        src_ref=crossing,
        dst_ref=crossed,
        send_sem=link_send.at[4],
        recv_sem=link_recv.at[4],
        device_id={"dp": across},
        device_id_type=MESH,
    )
    cross.start()
    for side, copy in near:
        if side == 0:
            copy.wait_recv()
    for k in range(kept):
        for half, part in products(0, k):
            total[half, k] = part
    for copy in sent:
        copy.wait_recv()
    cross.wait_recv()
    for k in range(kept):
        for half, right in enumerate((rel, rcl)):
            left = rxy[:, k, pl.ds(16 * half, 16)].reshape(n_dp * 16, BLOCK)
            part = dot_rows(left, right[:, k].reshape(n_dp * 16, BLOCK))
            grad = total[half, k] + crossed[half, k].astype(F32) + part
            grads_out[half, k] = (grad * scale).astype(BF16)

    for copy in sent + [copy for _, copy in near] + [cross]:
        copy.wait_send()
    g_copy.wait_send()
    v_copy.wait_send()
    g_end.wait()
    v_end.wait()


def hand_out(v, g, grads, values, score, tangent, adjoint, up, down, sem):
    moves = ((v, 0, values), (v, 1, tangent), (g, 0, score), (g, 1, adjoint), (grads, 0, up), (grads, 1, down))
    copies = [
        pltpu.make_async_copy(source.at[half], target.at[0], sem.at[n])
        for n, (source, half, target) in enumerate(moves)
    ]
    for copy in copies:
        copy.start()
    for copy in copies:
        copy.wait()


def on_device(mesh_shape, *arrays):
    (w_up, up_index, w_down, down_index, tick_order, *rest) = arrays
    n_section, n_dp = mesh_shape["section"], mesh_shape["dp"]
    blocks = w_up.shape[1]
    rows, width = rest[0].shape[1:]
    kept = blocks // n_dp
    smem = pl.BlockSpec(memory_space=pltpu.SMEM)
    hbm = pl.BlockSpec(memory_space=pltpu.HBM)
    vmem = pl.BlockSpec(memory_space=pltpu.VMEM)

    def by_block(height, copies=1):
        return pltpu.VMEM((copies * blocks, height, BLOCK), BF16)

    v, g, grads = pl.pallas_call(
        functools.partial(tick_kernel, n_section, n_dp, blocks, 1.0 / (rows * n_dp)),
        out_shape=(
            pltpu.VMEM((2, rows, width), BF16),
            pltpu.VMEM((2, rows, width), BF16),
            pltpu.VMEM((2, kept, BLOCK, BLOCK), BF16),
        ),
        in_specs=[smem] * 3 + [vmem] * 2 + [hbm] * 11,
        out_specs=(vmem, vmem, vmem),
        scratch_shapes=[
            pltpu.VMEM((blocks, BLOCK, BLOCK), BF16),
            pltpu.VMEM((blocks, BLOCK, BLOCK), BF16),
            pltpu.VMEM((2, 32, width), BF16),
            pltpu.VMEM((16, width), BF16),
            pltpu.VMEM((32, width), BF16),
            by_block(32, 2),
            by_block(8, 2),
            by_block(32),
            by_block(32),
            by_block(32),
            *[by_block(16)] * 5,
            *[pltpu.VMEM((2, 8, width), BF16)] * 2,
            by_block(32),
            by_block(48),
            by_block(32),
            *[by_block(16)] * 3,
            by_block(32),
            *[pltpu.VMEM((2, n_dp // 2, kept, 32, BLOCK), BF16)] * 4,
            pltpu.VMEM((n_dp, kept, 32, BLOCK), BF16),
            *[pltpu.VMEM((n_dp, kept, 16, BLOCK), BF16)] * 2,
            *[pltpu.VMEM((2, kept, BLOCK, BLOCK), BF16)] * 2,
            pltpu.VMEM((2, kept, BLOCK, BLOCK), F32),
            pltpu.VMEM((blocks + 1, 32, BLOCK), F32),
            pltpu.VMEM((blocks + 1, 16, BLOCK), F32),
            pltpu.VMEM((blocks, 32, BLOCK), F32),
            pltpu.VMEM((4, blocks), jnp.int32),
            pltpu.SMEM((4, blocks), jnp.int32),
            pltpu.SemaphoreType.DMA((17,)),
            *[pltpu.SemaphoreType.DMA((4, 2, len(ALONG_X)))] * 2,
            *[pltpu.SemaphoreType.DMA((3, n_dp - 1))] * 2,
            *[pltpu.SemaphoreType.DMA((5,))] * 2,
        ],
        compiler_params=pltpu.CompilerParams(
            collective_id=0, has_side_effects=True, vmem_limit_bytes=56 << 20
        ),
        name="ticks",
    )(up_index, down_index, tick_order, up_index, down_index, w_up, w_down, *rest)
    stream = jax.ShapeDtypeStruct((1, rows, width), BF16)
    grad = jax.ShapeDtypeStruct((1, kept, BLOCK, BLOCK), BF16)
    return pl.pallas_call(
        hand_out,
        out_shape=(stream,) * 4 + (grad,) * 2,
        in_specs=[vmem] * 3,
        out_specs=(hbm,) * 6,
        scratch_shapes=[pltpu.SemaphoreType.DMA((6,))],
        compiler_params=pltpu.CompilerParams(vmem_limit_bytes=8 << 20),
        name="hand_out",
    )(v, g, grads)


def solution(mesh):
    matrix = P("section", None, None, None)
    table = P("section", None)
    stream = P("section", "dp", None)
    saved = P("section", None, "dp", None)
    return jax.shard_map(
        functools.partial(on_device, dict(mesh.shape)),
        mesh=mesh,
        in_specs=(matrix, table, matrix, table, table) + (stream,) * 4 + (saved,) * 5,
        out_specs=(stream,) * 4 + (P("section", "dp", None, None),) * 2,
        check_vma=False,
    )
```

```python
import functools

import jax
import jax.numpy as jnp
from jax import lax
from jax.experimental import pallas as pl
from jax.experimental.pallas import tpu as pltpu
from jax.sharding import PartitionSpec as P

BLOCK = 128
UNROLL = 32
ALONG_X = (2, 1, 3)
FAR_FIRST = ((2, 1), (2, 0), (1, 1), (1, 0), (3, 1), (3, 0), (0, 1))
MESH = pl.DeviceIdType.MESH
F32 = jnp.float32
BF16 = jnp.bfloat16


def logistic(z):
    return 0.5 * jnp.tanh(0.5 * z) + 0.5


def silu_of(z, sig):
    return z * sig


def slope_of(z, sig):
    return sig * (1.0 + z * (1.0 - sig))


def curve_of(z, sig):
    return sig * (1.0 - sig) * (2.0 + z * (1.0 - 2.0 * sig))


def cols(i, width=BLOCK):
    return pl.ds(pl.multiple_of(i * width, width), width)


def each_block(count, body):
    def step(i, carry):
        body(i)
        return carry

    lax.fori_loop(0, count, step, 0, unroll=UNROLL)


def dot(a, b):
    return jnp.dot(a, b, preferred_element_type=F32)


def dot_rows(a, b):
    return lax.dot_general(a, b, (((0,), (0,)), ((), ())), preferred_element_type=F32)


def dot_t(a, b):
    return lax.dot_general(a, b, (((1,), (1,)), ((), ())), preferred_element_type=F32)


def tick_kernel(
    n_section, n_dp, blocks, scale,
    up_index, down_index, tick_order, up_row, down_row,
    w_up, w_down, values_in, score_in, tangent_in, adjoint_in,
    saved_back, saved_tan, saved_second, saved_second_tan, saved_second_grad,
    v_out, g_out, grads_out,
    wu, wd, raw_x, raw_v, raw_c, x_slots, c_slots, xt, xs, cs,
    v0, v1, g1, v_sent, g_sent, v_last, g_last,
    ys, yy, e0, e1, h0, h1, xl, yl, rx, rc, ry, re, rxl, ryl, rcl, rel, crossing, crossed, total,
    chain, chain2, keep, links_row, links,
    in_sem, near_send, near_recv, send_sem, recv_sem, link_send, link_recv,
):
    section = lax.axis_index("section")
    me = lax.axis_index("dp")
    after = lax.rem(section + 1, n_section)
    before = lax.rem(section + n_section - 1, n_section)
    kept = blocks // n_dp
    row = n_dp // 2
    my_x, my_y = me % row, me // row
    across = (1 - my_y) * row + my_x

    barrier = pltpu.get_barrier_semaphore()
    for p in range(1, n_dp):
        pl.semaphore_signal(barrier, inc=1, device_id={"dp": lax.rem(me + p, n_dp)}, device_id_type=MESH)
    for s in (after, before):
        pl.semaphore_signal(barrier, inc=1, device_id={"section": s}, device_id_type=MESH)

    loads = []

    def load(source, target):
        copy = pltpu.make_async_copy(source, target, in_sem.at[len(loads)])
        copy.start()
        loads.append(copy)

    for slot in range(2):
        for at, saved in enumerate((saved_back, saved_second, saved_second_tan, saved_tan)):
            load(saved.at[0, slot], raw_x.at[slot, pl.ds(8 * at, 8)])
    load(score_in.at[0], raw_c.at[pl.ds(0, 8)])
    load(adjoint_in.at[0], raw_c.at[pl.ds(8, 8)])
    for slot in range(2):
        load(saved_second_grad.at[0, slot], raw_c.at[pl.ds(16 + 8 * slot, 8)])
    early = len(loads)
    load(values_in.at[0], raw_v.at[pl.ds(0, 8)])
    load(tangent_in.at[0], raw_v.at[pl.ds(8, 8)])
    load(w_down.at[0], wd)
    load(w_up.at[0], wu)

    rows = lax.broadcasted_iota(jnp.int32, (blocks, blocks), 0)
    lanes = lax.broadcasted_iota(jnp.int32, (blocks, blocks), 1)
    for at, index in enumerate((down_row, up_row)):
        over = jnp.broadcast_to(index[...], (blocks, blocks))
        down = jnp.max(jnp.where(rows == lanes, over, 0), axis=1, keepdims=True)
        same = (down == over) & (rows < lanes)
        links_row[pl.ds(at, 1)] = jnp.max(jnp.where(same, rows + 1, 0), axis=0, keepdims=True)
        links_row[pl.ds(2 + at, 1)] = jnp.max(jnp.where(down == lanes, rows + 1, 0), axis=0, keepdims=True)
    links_copy = pltpu.make_async_copy(links_row, links, in_sem.at[len(loads)])
    links_copy.start()

    first = tick_order[0, 0] * blocks
    later = tick_order[0, 1] * blocks

    chain[0] = jnp.zeros(chain.shape[1:], F32)
    chain2[0] = jnp.zeros(chain2.shape[1:], F32)

    for copy in loads[:early]:
        copy.wait()

    def to_blocks(j):
        here = cols(j)
        for slot in range(2):
            x_slots[slot * blocks + j] = raw_x[slot, :, here]
            c_slots[slot * blocks + j] = raw_c[pl.ds(16 + 8 * slot, 8), here]
        cs[j, pl.ds(0, 16)] = raw_c[pl.ds(0, 16), here]

    each_block(blocks, to_blocks)

    def gather_x(j):
        source = up_index[0, j]
        xs[j, pl.ds(0, 24)] = x_slots[first + source, pl.ds(0, 24)]
        xs[j, pl.ds(24, 8)] = x_slots[later + source, pl.ds(16, 8)]
        xl[j] = x_slots[later + source, pl.ds(0, 16)]
        cs[j, pl.ds(16, 8)] = c_slots[first + j]
        cs[j, pl.ds(24, 8)] = c_slots[later + j]

    each_block(blocks, gather_x)
    pl.semaphore_wait(barrier, n_dp + 1)

    sent = []

    near = []

    def slab(ref, d):
        return ref.at[pl.ds(d * kept, kept)]

    def spread_near(*parts):
        for side in (1, 0):
            for kind, source, landing in parts:
                for n, dx in enumerate(ALONG_X):
                    x = (my_x + dx) % row
                    peer = my_y * row + x
                    keeper = (my_y if side == 0 else 1 - my_y) * row + x
                    copy = pltpu.make_async_remote_copy(
                        src_ref=slab(source, keeper),
                        dst_ref=landing.at[side, my_x],
                        send_sem=near_send.at[kind, side, n],
                        recv_sem=near_recv.at[kind, side, n],
                        device_id={"dp": peer},
                        device_id_type=MESH,
                    )
                    copy.start()
                    near.append((side, copy))
        for kind, source, landing in parts:
            landing[0, my_x] = source[pl.ds(me * kept, kept)]
            landing[1, my_x] = source[pl.ds(across * kept, kept)]

    def spread(kind, source, landing):
        for n, (dx, dy) in enumerate(FAR_FIRST):
            peer = (my_y + dy) % 2 * row + (my_x + dx) % row
            copy = pltpu.make_async_remote_copy(
                src_ref=slab(source, peer),
                dst_ref=landing.at[me],
                send_sem=send_sem.at[kind, n],
                recv_sem=recv_sem.at[kind, n],
                device_id={"dp": peer},
                device_id_type=MESH,
            )
            copy.start()
            sent.append(copy)
        landing[me] = source[pl.ds(me * kept, kept)]

    spread(0, xl, rxl)
    spread_near((0, xs, rx), (1, cs, rc))

    for copy in loads[early : early + 2]:
        copy.wait()

    def to_blocks_v(j):
        v0[j] = raw_v[:, cols(j)]

    each_block(blocks, to_blocks_v)

    def gather_v(j):
        source = up_index[0, j]
        xt[j, pl.ds(0, 16)] = v0[source]
        xt[j, pl.ds(16, 8)] = x_slots[first + source, pl.ds(24, 8)]
        xt[j, pl.ds(24, 8)] = x_slots[later + source, pl.ds(24, 8)]

    each_block(blocks, gather_v)
    links_copy.wait()
    loads[early + 2].wait()

    def pull(i):
        chain[i + 1] = dot_t(cs[i], wd[i]) + chain[links[0, i]]

    each_block(blocks, pull)
    loads[early + 3].wait()

    def raise_first(j):
        z = dot(jnp.concatenate([xt[j, pl.ds(0, 24)], xs[j, pl.ds(0, 24)]], 0), wu[j])
        zv, zt, tan, back, za, ta = (z[8 * n : 8 * n + 8] for n in range(6))
        pulled = chain[links[2, j]]
        pg, pa, ps = pulled[0:8], pulled[8:16], pulled[16:24]
        sig, sig_back = logistic(za), logistic(back)
        slope = slope_of(za, sig)
        hidden = silu_of(zv, logistic(zv))
        tangent_hidden = slope_of(tan, logistic(tan)) * zt
        h0[j] = jnp.concatenate([hidden, tangent_hidden], 0).astype(BF16)
        gate = slope_of(back, sig_back) * pg
        push = slope * pa + curve_of(za, sig) * ps * ta
        e0[j, pl.ds(0, 16)] = jnp.concatenate([gate, push], 0).astype(BF16)
        e0[j, pl.ds(16, 8)] = (slope * ps).astype(BF16)
        yy[j, pl.ds(0, 16)] = jnp.concatenate([silu_of(back, sig_back), silu_of(za, sig)], 0).astype(BF16)
        yy[j, pl.ds(16, 8)] = (slope * ta).astype(BF16)

    each_block(blocks, raise_first)

    def raise_saved(j):
        rows = jnp.concatenate([xt[j, pl.ds(24, 8)], xs[j, pl.ds(24, 8)], xl[j]], 0)
        z = dot(rows, wu[j])
        tan, ta, back, za = (z[8 * n : 8 * n + 8] for n in range(4))
        ps = chain[links[2, j], pl.ds(24, 8)]
        sig, sig_back = logistic(za), logistic(back)
        slope = slope_of(za, sig)
        e0[j, pl.ds(24, 8)] = (slope * ps).astype(BF16)
        yy[j, pl.ds(24, 8)] = (slope * ta).astype(BF16)
        yy[j, pl.ds(32, 16)] = jnp.concatenate([silu_of(back, sig_back), silu_of(za, sig)], 0).astype(BF16)
        keep[j] = jnp.concatenate(
            [slope_of(back, sig_back), slope, curve_of(za, sig) * ps * ta, slope_of(tan, logistic(tan))], 0
        )

    def push_back(source):
        def body(j):
            chain2[j + 1] = dot_t(source[j, pl.ds(0, 16)], wu[j]) + chain2[links[1, j]]

        each_block(blocks, body)

    def settle(source, put):
        def body(b):
            put(b, (source[b, pl.ds(0, 16)].astype(F32) + chain2[links[3, b]]).astype(BF16))

        each_block(blocks, body)

    def lower(hidden, source, put):
        def body(i):
            put(i, (source[i].astype(F32) + dot(hidden[down_index[0, i]], wd[i])).astype(BF16))

        each_block(blocks, body)

    def in_block(ref):
        def put(i, value):
            ref[i] = value

        return put

    def in_rows(ref):
        def put(i, value):
            ref[0, :, cols(i)] = value[0:8]
            ref[1, :, cols(i)] = value[8:16]

        return put

    def relay(kind, source, landing, to):
        copy = pltpu.make_async_remote_copy(
            src_ref=source,
            dst_ref=landing,
            send_sem=link_send.at[kind],
            recv_sem=link_recv.at[kind],
            device_id={"section": to},
            device_id_type=MESH,
        )
        copy.start()
        return copy

    push_back(e0)
    settle(cs, in_block(g_sent))
    g_copy = relay(0, g_sent, g1, before)
    lower(h0, v0, in_block(v_sent))
    v_copy = relay(1, v_sent, v1, after)

    each_block(blocks, raise_saved)

    def gather_y(i):
        source = down_index[0, i]
        ys[i] = yy[source, pl.ds(0, 32)]
        yl[i] = yy[source, pl.ds(32, 16)]

    each_block(blocks, gather_y)
    spread_near((2, ys, ry), (3, e0, re))
    spread(3, yl, ryl)

    g_copy.wait_recv()

    def pull_later(i):
        chain[i + 1, pl.ds(0, 16)] = dot_t(g1[i], wd[i]) + chain[links[0, i], pl.ds(0, 16)]

    each_block(blocks, pull_later)

    def gate_later(j):
        pulled = chain[links[2, j], pl.ds(0, 16)]
        kept_rows = keep[j]
        gate = kept_rows[0:8] * pulled[0:8]
        push = kept_rows[8:16] * pulled[8:16] + kept_rows[16:24]
        e1[j] = jnp.concatenate([gate, push], 0).astype(BF16)

    each_block(blocks, gate_later)

    push_back(e1)
    settle(g1, in_rows(g_last))
    g_end = relay(2, g_last, g_out, before)
    spread(1, g1, rcl)
    spread(2, e1, rel)

    v_copy.wait_recv()

    def raise_later(j):
        z = dot(v1[up_index[0, j]], wu[j])
        zv, zt = z[0:8], z[8:16]
        h1[j] = jnp.concatenate([silu_of(zv, logistic(zv)), keep[j, pl.ds(24, 8)] * zt], 0).astype(BF16)

    each_block(blocks, raise_later)
    lower(h1, v1, in_rows(v_last))
    v_end = relay(3, v_last, v_out, after)

    def products(side, k):
        for half, (left, right) in enumerate(((rx, re), (ry, rc))):
            yield half, dot_rows(left[side, :, k].reshape(row * 32, BLOCK), right[side, :, k].reshape(row * 32, BLOCK))

    for side, copy in near:
        if side == 1:
            copy.wait_recv()
    for k in range(kept):
        for half, part in products(1, k):
            crossing[half, k] = part.astype(BF16)
    cross = pltpu.make_async_remote_copy(
        src_ref=crossing,
        dst_ref=crossed,
        send_sem=link_send.at[4],
        recv_sem=link_recv.at[4],
        device_id={"dp": across},
        device_id_type=MESH,
    )
    cross.start()
    for side, copy in near:
        if side == 0:
            copy.wait_recv()
    for k in range(kept):
        for half, part in products(0, k):
            total[half, k] = part
    for copy in sent:
        copy.wait_recv()
    cross.wait_recv()
    for k in range(kept):
        for half, (left, right) in enumerate(((rxl, rel), (ryl, rcl))):
            part = dot_rows(left[:, k].reshape(n_dp * 16, BLOCK), right[:, k].reshape(n_dp * 16, BLOCK))
            grad = total[half, k] + crossed[half, k].astype(F32) + part
            grads_out[half, k] = (grad * scale).astype(BF16)

    for copy in sent + [copy for _, copy in near] + [cross]:
        copy.wait_send()
    g_copy.wait_send()
    v_copy.wait_send()
    g_end.wait()
    v_end.wait()


def hand_out(v, g, grads, values, score, tangent, adjoint, up, down, sem):
    moves = ((v, 0, values), (v, 1, tangent), (g, 0, score), (g, 1, adjoint), (grads, 0, up), (grads, 1, down))
    copies = [
        pltpu.make_async_copy(source.at[half], target.at[0], sem.at[n])
        for n, (source, half, target) in enumerate(moves)
    ]
    for copy in copies:
        copy.start()
    for copy in copies:
        copy.wait()


def on_device(mesh_shape, *arrays):
    (w_up, up_index, w_down, down_index, tick_order, *rest) = arrays
    n_section, n_dp = mesh_shape["section"], mesh_shape["dp"]
    blocks = w_up.shape[1]
    rows, width = rest[0].shape[1:]
    kept = blocks // n_dp
    smem = pl.BlockSpec(memory_space=pltpu.SMEM)
    hbm = pl.BlockSpec(memory_space=pltpu.HBM)
    vmem = pl.BlockSpec(memory_space=pltpu.VMEM)

    def by_block(height, copies=1):
        return pltpu.VMEM((copies * blocks, height, BLOCK), BF16)

    v, g, grads = pl.pallas_call(
        functools.partial(tick_kernel, n_section, n_dp, blocks, 1.0 / (rows * n_dp)),
        out_shape=(
            pltpu.VMEM((2, rows, width), BF16),
            pltpu.VMEM((2, rows, width), BF16),
            pltpu.VMEM((2, kept, BLOCK, BLOCK), BF16),
        ),
        in_specs=[smem] * 3 + [vmem] * 2 + [hbm] * 11,
        out_specs=(vmem, vmem, vmem),
        scratch_shapes=[
            pltpu.VMEM((blocks, BLOCK, BLOCK), BF16),
            pltpu.VMEM((blocks, BLOCK, BLOCK), BF16),
            pltpu.VMEM((2, 32, width), BF16),
            pltpu.VMEM((16, width), BF16),
            pltpu.VMEM((32, width), BF16),
            by_block(32, 2),
            by_block(8, 2),
            by_block(32),
            by_block(32),
            by_block(32),
            *[by_block(16)] * 5,
            *[pltpu.VMEM((2, 8, width), BF16)] * 2,
            by_block(32),
            by_block(48),
            by_block(32),
            *[by_block(16)] * 5,
            *[pltpu.VMEM((2, n_dp // 2, kept, 32, BLOCK), BF16)] * 4,
            *[pltpu.VMEM((n_dp, kept, 16, BLOCK), BF16)] * 4,
            *[pltpu.VMEM((2, kept, BLOCK, BLOCK), BF16)] * 2,
            pltpu.VMEM((2, kept, BLOCK, BLOCK), F32),
            pltpu.VMEM((blocks + 1, 32, BLOCK), F32),
            pltpu.VMEM((blocks + 1, 16, BLOCK), F32),
            pltpu.VMEM((blocks, 32, BLOCK), F32),
            pltpu.VMEM((4, blocks), jnp.int32),
            pltpu.SMEM((4, blocks), jnp.int32),
            pltpu.SemaphoreType.DMA((17,)),
            *[pltpu.SemaphoreType.DMA((4, 2, len(ALONG_X)))] * 2,
            *[pltpu.SemaphoreType.DMA((4, n_dp - 1))] * 2,
            *[pltpu.SemaphoreType.DMA((5,))] * 2,
        ],
        compiler_params=pltpu.CompilerParams(
            collective_id=0, has_side_effects=True, vmem_limit_bytes=56 << 20
        ),
        name="ticks",
    )(up_index, down_index, tick_order, up_index, down_index, w_up, w_down, *rest)
    stream = jax.ShapeDtypeStruct((1, rows, width), BF16)
    grad = jax.ShapeDtypeStruct((1, kept, BLOCK, BLOCK), BF16)
    return pl.pallas_call(
        hand_out,
        out_shape=(stream,) * 4 + (grad,) * 2,
        in_specs=[vmem] * 3,
        out_specs=(hbm,) * 6,
        scratch_shapes=[pltpu.SemaphoreType.DMA((6,))],
        compiler_params=pltpu.CompilerParams(vmem_limit_bytes=8 << 20),
        name="hand_out",
    )(v, g, grads)


def solution(mesh):
    matrix = P("section", None, None, None)
    table = P("section", None)
    stream = P("section", "dp", None)
    saved = P("section", None, "dp", None)
    return jax.shard_map(
        functools.partial(on_device, dict(mesh.shape)),
        mesh=mesh,
        in_specs=(matrix, table, matrix, table, table) + (stream,) * 4 + (saved,) * 5,
        out_specs=(stream,) * 4 + (P("section", "dp", None, None),) * 2,
        check_vma=False,
    )
```
